32 devices in a mesh: fsdp: 8 (over z, x), seq: 2 (over core), replica: 2 (over y).
Axes of the slice: x: 2, y: 2, z: 4, core: 2. Of those that a mesh axis runs over, the one named last changes fastest.
Arguments:
- clips_in: bfloat16 [16, 448, 1024], P(('fsdp', 'replica'), 'seq'), may hold values from -6 to 6
- cotangent: bfloat16 [16, 448, 1024], P(('fsdp', 'replica'), 'seq'), may hold values from -6 to 6
- clip_mask: int32 [16], P(('fsdp', 'replica')), may hold values 0 or 1
- norm1_gain: bfloat16 [2, 1024], P(None, ('fsdp', 'seq')), may hold values from 0.25 to 1.75
- norm1_bias: bfloat16 [2, 1024], P(None, ('fsdp', 'seq')), may hold values from -1.5 to 1.5
- qkv_weight: bfloat16 [2, 1024, 3072], P(None, ('fsdp', 'seq')), may hold values from -0.1875 to 0.1875
- query_bias: bfloat16 [2, 1024], P(None, ('fsdp', 'seq')), may hold values from -1.5 to 1.5
- value_bias: bfloat16 [2, 1024], P(None, ('fsdp', 'seq')), may hold values from -0.25 to 0.25
- proj_weight: bfloat16 [2, 1024, 1024], P(None, ('fsdp', 'seq')), may hold values from -2 to 2
- proj_bias: bfloat16 [2, 1024], P(None, ('fsdp', 'seq')), may hold values from -1.5 to 1.5
- norm2_gain: bfloat16 [2, 1024], P(None, ('fsdp', 'seq')), may hold values from 0.25 to 1.75
- norm2_bias: bfloat16 [2, 1024], P(None, ('fsdp', 'seq')), may hold values from -1.5 to 1.5
- up_weight: bfloat16 [2, 1024, 4096], P(None, ('fsdp', 'seq')), may hold values from -0.1875 to 0.1875
- up_bias: bfloat16 [2, 4096], P(None, ('fsdp', 'seq')), may hold values from -1.5 to 1.5
- down_weight: bfloat16 [2, 4096, 1024], P(None, ('fsdp', 'seq')), may hold values from -0.09375 to 0.09375
- down_bias: bfloat16 [2, 1024], P(None, ('fsdp', 'seq')), may hold values from -1.5 to 1.5
Outputs:
- clips_out: bfloat16 [16, 448, 1024], P(('fsdp', 'replica'), 'seq')
- input_grad: float32 [16, 448, 1024], P(('fsdp', 'replica'), 'seq')
- grad_norm1_gain: float32 [2, 1024], P(None, ('fsdp', 'seq'))
- grad_norm1_bias: float32 [2, 1024], P(None, ('fsdp', 'seq'))
- grad_qkv_weight: float32 [2, 1024, 3072], P(None, ('fsdp', 'seq'))
- grad_query_bias: float32 [2, 1024], P(None, ('fsdp', 'seq'))
- grad_value_bias: float32 [2, 1024], P(None, ('fsdp', 'seq'))
- grad_proj_weight: float32 [2, 1024, 1024], P(None, ('fsdp', 'seq'))
- grad_proj_bias: float32 [2, 1024], P(None, ('fsdp', 'seq'))
- grad_norm2_gain: float32 [2, 1024], P(None, ('fsdp', 'seq'))
- grad_norm2_bias: float32 [2, 1024], P(None, ('fsdp', 'seq'))
- grad_up_weight: float32 [2, 1024, 4096], P(None, ('fsdp', 'seq'))
- grad_up_bias: float32 [2, 4096], P(None, ('fsdp', 'seq'))
- grad_down_weight: float32 [2, 4096, 1024], P(None, ('fsdp', 'seq'))
- grad_down_bias: float32 [2, 1024], P(None, ('fsdp', 'seq'))
The draws below stay inside these ranges and needn't reach their ends.
All inputs are finite; a program needn't handle non-finite values. No bound on the sum of `clip_mask` on one device may be relied on, other than what follows from the above.
Results may differ from the reference program's by a relative error of at most 0.013.
Values may be sent and summed in bfloat16 or wider, within the bound.
No kernel may reach another device: no remote copies, remote signals or barrier semaphores. Data moves between devices by JAX's collectives and lax.ppermute only.
A program may use at most 256 MiB of HBM per device.

```python
import jax
import jax.numpy as jnp
from jax import lax

D = 1024
HEADS = 16
FF = 4096
LAYERS = 2
CLIP_TOK = 448
CLIPS = 16


def with_ends(array, own_key, low, high):
    extent = array.shape
    spot = [jax.random.randint(jax.random.fold_in(own_key, axis), (), 0, extent[axis]) for axis in range(len(extent))]
    array = array.at[tuple(spot)].set(low)
    longest = extent.index(max(extent))
    spot[longest] = (spot[longest] + 1) % extent[longest]
    return array.at[tuple(spot)].set(high)


def levels(stream_key, dims, split, low, high):
    factor_of, own = 1.0, jax.random.fold_in(stream_key, 6)
    for dim, blocks in split:
        steps = jnp.exp(jax.random.uniform(jax.random.fold_in(own, dim), (blocks,), jnp.float32, low / len(split), high / len(split)))
        factor_of = factor_of * jnp.repeat(steps, dims[dim] // blocks).reshape([-1 if axis == dim else 1 for axis in range(len(dims))])
    return factor_of


def centred(own_key, shape, scale, limit, pieces=(), dtype=jnp.bfloat16):
    entries = scale * jax.random.normal(own_key, shape, jnp.float32)
    if pieces:
        entries = entries * levels(own_key, shape, pieces, -0.22, 0.18)
    return jnp.clip(entries, -limit, limit).astype(dtype)


def setup_inputs(seed: int = 0) -> dict:
    key_list = jax.random.split(jax.random.key(seed), 17)
    return {
        "clips_in": centred(key_list[0], (CLIPS, CLIP_TOK, D), 1.0, 6.0, ((0, 16), (1, 2))),
        "cotangent": centred(key_list[1], (CLIPS, CLIP_TOK, D), 1.0, 6.0, ((0, 16), (1, 2))),
        "clip_mask": with_ends((jax.random.randint(key_list[2], (CLIPS,), 0, 4) < 3).astype(jnp.int32), jax.random.fold_in(key_list[2], 1), 0, 1),
        "norm1_gain": jnp.clip(1.0 + 0.15 * jax.random.normal(key_list[3], (LAYERS, D), jnp.float32), 0.25, 1.75).astype(jnp.bfloat16),
        "norm1_bias": centred(key_list[4], (LAYERS, D), 0.3, 1.5, ((1, 16),)),
        "qkv_weight": centred(key_list[5], (LAYERS, D, 3 * D), D ** -0.5, 0.1875, ((1, 16),)),
        "query_bias": centred(key_list[6], (LAYERS, D), 0.3, 1.5, ((1, 16),)),
        "value_bias": centred(key_list[7], (LAYERS, D), 0.05, 0.25, ((1, 16),)),
        "proj_weight": centred(key_list[8], (LAYERS, D, D), (D * 4 // CLIP_TOK) ** -0.5, 2.0, ((1, 16),)),
        "proj_bias": centred(key_list[9], (LAYERS, D), 0.3, 1.5, ((1, 16),)),
        "norm2_gain": jnp.clip(1.0 + 0.15 * jax.random.normal(key_list[10], (LAYERS, D), jnp.float32), 0.25, 1.75).astype(jnp.bfloat16),
        "norm2_bias": centred(key_list[11], (LAYERS, D), 0.3, 1.5, ((1, 16),)),
        "up_weight": centred(key_list[12], (LAYERS, D, FF), D ** -0.5, 0.1875, ((1, 16),)),
        "up_bias": centred(key_list[13], (LAYERS, FF), 0.3, 1.5, ((1, 16),)),
        "down_weight": centred(key_list[14], (LAYERS, FF, D), FF ** -0.5, 0.09375, ((1, 16),)),
        "down_bias": centred(key_list[15], (LAYERS, D), 0.3, 1.5, ((1, 16),)),
    }


norm_eps = 1e-06
highest = lax.Precision.HIGHEST

@jax.custom_vjp
def low(v):
    return lax.optimization_barrier(v.astype(jnp.bfloat16)).astype(jnp.float32)

@jax.custom_vjp
def low_back(v):
    return v

def low_keep(v):
    return (low(v), None)

def low_pass(kept, grad):
    return (grad,)

def back_keep(v):
    return (v, None)

def back_low(kept, grad):
    return (low(grad),)
low.defvjp(low_keep, low_pass)
low_back.defvjp(back_keep, back_low)

def layer_norm(inputs, gain, shift):
    center = inputs - lax.optimization_barrier(jnp.mean(inputs, axis=-1, keepdims=True))
    spread = lax.optimization_barrier(jnp.mean(center * center, axis=-1, keepdims=True))
    return center * lax.rsqrt(spread + norm_eps) * gain + shift

def exact_gelu(inputs):
    return jax.nn.gelu(inputs, approximate=False)

def block_forward(resid, weights):
    gain_one, shift_one, qkv_weight, query_bias, value_bias, proj_weight, proj_bias, gain_two, shift_two, up_weight, up_bias, down_weight, down_bias = weights
    tok_count, width = resid.shape
    head_size = width // HEADS
    normed = low(layer_norm(resid, gain_one, shift_one))
    joined = jnp.dot(normed, qkv_weight, precision=highest)
    queries = low(low_back((joined[:, :width] + query_bias) * 0.125)).reshape(tok_count, HEADS, head_size)
    keys = low(low_back(joined[:, width:2 * width])).reshape(tok_count, HEADS, head_size)
    values = low(low_back(joined[:, 2 * width:] + value_bias)).reshape(tok_count, HEADS, head_size)
    scores = low_back(jnp.einsum('qhd,khd->hqk', queries, keys, precision=highest))
    probs = low(jax.nn.softmax(scores, axis=-1))
    attended = jnp.einsum('hqk,khd->qhd', probs, values, precision=highest).reshape(tok_count, width)
    attended = low(low_back(attended))
    mid = resid + low_back(jnp.dot(attended, proj_weight, precision=highest) + proj_bias)
    normed_two = low(layer_norm(mid, gain_two, shift_two))
    pre = low_back(jnp.dot(normed_two, up_weight, precision=highest) + up_bias)
    active = low(exact_gelu(pre))
    return mid + low_back(jnp.dot(active, down_weight, precision=highest) + down_bias)

def reference(clips_in, cotangent, clip_mask, norm1_gain, norm1_bias, qkv_weight, query_bias, value_bias, proj_weight, proj_bias, norm2_gain, norm2_bias, up_weight, up_bias, down_weight, down_bias):
    params = tuple((weight.astype(jnp.float32) for weight in (norm1_gain, norm1_bias, qkv_weight, query_bias, value_bias, proj_weight, proj_bias, norm2_gain, norm2_bias, up_weight, up_bias, down_weight, down_bias)))

    def model(clip, weights):
        resid = clip
        for layer_at in range(LAYERS):
            resid = block_forward(resid, tuple((weight[layer_at] for weight in weights)))
        return resid

    def per_clip(totals, item):
        clip, seed_grad, flag = item
        result, pull = jax.vjp(model, clip.astype(jnp.float32), params)
        d_input, d_params = pull(seed_grad.astype(jnp.float32) * flag.astype(jnp.float32))
        totals = jax.tree.map(jnp.add, totals, d_params)
        return (totals, (result.astype(jnp.bfloat16), d_input))
    zeros = jax.tree.map(jnp.zeros_like, params)
    totals, (outputs, input_grads) = lax.scan(per_clip, zeros, (clips_in, cotangent, clip_mask))
    return (outputs, input_grads, totals[0], totals[1], totals[2], totals[3], totals[4], totals[5], totals[6], totals[7], totals[8], totals[9], totals[10], totals[11], totals[12])
```

```python
import functools

import jax
import jax.numpy as jnp
from jax import lax
from jax.experimental import pallas as pl
from jax.experimental.pallas import tpu as pltpu
from jax.sharding import PartitionSpec as P


HEADS = 16
LAYERS = 2
norm_eps = 1e-06
bf16 = jnp.bfloat16
f32 = jnp.float32


def widen(array):
    return array.astype(f32)


def dot(a, b, dims):
    return lax.dot_general(a, b, (dims, ((), ())), preferred_element_type=f32)


def mm(a, b):
    return dot(a, b, ((1,), (0,)))


def mm_t(a, b):
    return dot(a, b, ((1,), (1,)))


def t_mm(a, b):
    return dot(a, b, ((0,), (0,)))


PAIR = [(0, 1), (1, 0)]


def core_swap(v):
    return lax.ppermute(v, "seq", PAIR)


def y_swap(v):
    return lax.ppermute(v, "replica", PAIR)


def x_swap(v, n):
    return lax.ppermute(v, "fsdp", [(f, f ^ 1) for f in range(n)])


def z_from(v, k, n):
    nz = n // 2
    return lax.ppermute(
        v, "fsdp", [(((z + k) % nz) * 2 + x, z * 2 + x) for z in range(nz) for x in range(2)]
    )


def pick(array, axis, at):
    return lax.dynamic_index_in_dim(array, at, axis, keepdims=False)


TILE = 32
COLS = 256
VMEM_LIMIT = 14 * 1024 * 1024


def call(body, outs, args, flops, transcendentals=0, scratch=()):
    touched = sum(a.size * a.dtype.itemsize for a in args)
    outs = tuple(jax.ShapeDtypeStruct(shape, dtype) for shape, dtype in outs)
    touched = touched + sum(o.size * o.dtype.itemsize for o in outs)
    return pl.pallas_call(
        body,
        out_shape=outs,
        scratch_shapes=list(scratch),
        compiler_params=pltpu.CompilerParams(vmem_limit_bytes=VMEM_LIMIT),
        cost_estimate=pl.CostEstimate(
            flops=flops, bytes_accessed=touched, transcendentals=transcendentals
        ),
    )(*args)


def norm_parts(inputs):
    center = inputs - jnp.mean(inputs, axis=-1, keepdims=True)
    spread = jnp.mean(center * center, axis=-1, keepdims=True)
    scale = lax.rsqrt(spread + norm_eps)
    return center * scale, scale


def norm_grad(e, inputs, gain):
    unit, scale = norm_parts(inputs)
    eg = e * gain
    d = scale * (
        eg
        - jnp.mean(eg, axis=-1, keepdims=True)
        - unit * jnp.mean(eg * unit, axis=-1, keepdims=True)
    )
    return d, e * unit


def eight(v):
    return jnp.sum(v.reshape(v.shape[0] // 8, 8, v.shape[1]), axis=0)


def by_rows(half_rows, step):
    for half in range(2):

        @pl.loop(0, half_rows // TILE)
        def _(i):
            start = pl.multiple_of(i * TILE, TILE)
            step(pl.ds(half * half_rows + start, TILE), half, pl.ds(start, TILE))


def by_cols(width, step):
    @pl.loop(0, width // COLS)
    def _(i):
        step(pl.ds(pl.multiple_of(i * COLS, COLS), COLS))


def summed(sent, whole, half, part):
    rows = sent[1].shape[0] // 2
    side = pl.ds((1 - half) * rows + part.start, TILE)
    total = sent[0][whole, :] + widen(sent[1][side, :])
    return total + widen(sent[2 + half][part, :])


def put_part(part_ref, low_ref, cols, value):
    part_ref[:, cols] = value
    low_ref[:, cols] = value.astype(bf16)


def heads_of(ref, width, size, h):
    return [ref[:, i * width + h * size : i * width + (h + 1) * size] for i in range(3)]


def attend_body(first, heads, size, *refs):
    if first:
        base, vec, w_qkv, fix, w_proj, normed, qkv, attended, part, low = refs
        sent = None
    else:
        base, s0, s1, s2, s3, vec, w_qkv, fix, w_proj = refs[:9]
        resid, normed, qkv, attended, part, low = refs[9:]
        sent = (s0, s1, s2, s3)
    width = heads * size

    def norm(whole, half, part_rows):
        value = widen(base[whole, :])
        if sent is not None:
            value = value + (summed(sent, whole, half, part_rows) + vec[2:3, :])
            resid[whole, :] = value
        unit, _ = norm_parts(value)
        normed[whole, :] = (unit * vec[0:1, :] + vec[1:2, :]).astype(bf16)

    by_rows(base.shape[0] // 2, norm)

    def project(cols):
        value = (mm(normed[...], w_qkv[:, cols]) + fix[0:1, cols]) * fix[1:2, cols]
        qkv[:, cols] = value.astype(bf16)

    by_cols(3 * width, project)
    for h in range(heads):
        q, k, v = heads_of(qkv, width, size, h)
        s = mm_t(q, k)
        e = jnp.exp(s - jnp.max(s, axis=-1, keepdims=True))
        p = (e / jnp.sum(e, axis=-1, keepdims=True)).astype(bf16)
        attended[:, h * size : (h + 1) * size] = mm(p, v).astype(bf16)
    by_cols(part.shape[1], lambda cols: put_part(part, low, cols, mm(attended[...], w_proj[:, cols])))


def attend(base, sent, vec, w_qkv, fix, w_proj, heads, size):
    toks, width = base.shape
    first = sent is None
    outs = [((toks, width), bf16), ((toks, 3 * heads * size), bf16)]
    outs = outs + [((toks, heads * size), bf16), ((toks, width), f32), ((toks, width), bf16)]
    if not first:
        outs = [((toks, width), f32)] + outs
    args = [base, *(sent or ()), vec, w_qkv, fix, w_proj]
    flops = 8 * toks * width * heads * size + 4 * heads * toks * toks * size
    got = call(
        functools.partial(attend_body, first, heads, size), outs, args, flops, heads * toks * toks
    )
    return got if not first else (base, *got)


ROOT_HALF = 0.7071067811865476
ROOT_TWO_PI_INV = 0.3989422804014327


def widen_body(base, s0, s1, s2, s3, vec, w_up, up_b, mid, normed, active, slope):
    sent = (s0, s1, s2, s3)

    def norm(whole, half, part_rows):
        value = widen(base[whole, :])
        value = value + (summed(sent, whole, half, part_rows) + vec[2:3, :])
        mid[whole, :] = value
        unit, _ = norm_parts(value)
        normed[whole, :] = (unit * vec[0:1, :] + vec[1:2, :]).astype(bf16)

    by_rows(base.shape[0] // 2, norm)

    def up(cols):
        pre = mm(normed[...], w_up[:, cols]) + up_b[:, cols]
        half = 0.5 * (1.0 + lax.erf(pre * ROOT_HALF))
        active[:, cols] = (pre * half).astype(bf16)
        slope[:, cols] = half + pre * (ROOT_TWO_PI_INV * jnp.exp(-0.5 * pre * pre))

    by_cols(w_up.shape[1], up)


def go_up(base, sent, vec, w_up, up_b):
    toks, width = base.shape
    hid = w_up.shape[1]
    outs = [((toks, width), f32), ((toks, width), bf16)]
    outs = outs + [((toks, hid), bf16), ((toks, hid), f32)]
    args = [base, *sent, vec, w_up, up_b]
    return call(widen_body, outs, args, 2 * toks * width * hid, toks * hid)


def down_body(active, w_down, part, low):
    by_cols(part.shape[1], lambda cols: put_part(part, low, cols, mm(active[...], w_down[:, cols])))


def go_down(active, w_down):
    shape = (active.shape[0], w_down.shape[1])
    flops = 2 * active.size * w_down.shape[1]
    return call(down_body, [(shape, f32), (shape, bf16)], [active, w_down], flops)


def mlp_back_tail(d_mlp, slope, w_down, w_up, d_pre, part, low, up_sum):
    def back(cols):
        value = (mm_t(d_mlp[...], w_down[cols, :]) * slope[:, cols]).astype(bf16)
        d_pre[:, cols] = value
        up_sum[:, cols] = eight(widen(value))

    by_cols(w_down.shape[0], back)
    by_cols(part.shape[1], lambda cols: put_part(part, low, cols, mm_t(d_pre[...], w_up[cols, :])))


def mlp_back_first(d_mlp, slope, w_down, w_up, d_pre, part, low, up_sum):
    mlp_back_tail(d_mlp, slope, w_down, w_up, d_pre, part, low, up_sum)


def mlp_back_body(base, d_mid, s0, s1, s2, s3, vec, slope, w_down, w_up, *outs):
    grad, d_mlp, d_pre, part, low, up_sum, sums = outs
    sums[...] = jnp.zeros_like(sums)

    def norm(whole, half, part_rows):
        e = summed((s0, s1, s2, s3), whole, half, part_rows)
        d, by_gain = norm_grad(e, widen(base[whole, :]), vec[0:1, :])
        value = d_mid[whole, :] + d
        grad[whole, :] = value
        low_value = value.astype(bf16)
        d_mlp[whole, :] = low_value
        sums[0:8, :] += eight(by_gain)
        sums[8:16, :] += eight(e)
        sums[16:24, :] += eight(widen(low_value))

    by_rows(base.shape[0] // 2, norm)
    mlp_back_tail(d_mlp, slope, w_down, w_up, d_pre, part, low, up_sum)


def mlp_back(first, base, d_mid, sent, vec, slope, w_down, w_up):
    toks, hid = slope.shape
    width = w_up.shape[0]
    outs = [((toks, hid), bf16), ((toks, width), f32), ((toks, width), bf16), ((8, hid), f32)]
    flops = 4 * toks * hid * width
    if first is not None:
        args = [first, slope, w_down, w_up]
        return call(mlp_back_first, outs, args, flops)
    outs = [((toks, width), f32), ((toks, width), bf16), *outs, ((24, width), f32)]
    args = [base, d_mid, *sent, vec, slope, w_down, w_up]
    return call(mlp_back_body, outs, args, flops)


def attend_back_body(heads, size, grad, mid, s0, s1, s2, s3, vec, qkv, w_proj, w_qkv, *refs):
    d_mid, d_branch, d_joined, part, low, sums, joined_sum, d_att = refs
    width = heads * size
    sums[...] = jnp.zeros_like(sums)

    def norm(whole, half, part_rows):
        e = summed((s0, s1, s2, s3), whole, half, part_rows)
        d, by_gain = norm_grad(e, mid[whole, :], vec[0:1, :])
        value = widen(grad[whole, :]) + d
        d_mid[whole, :] = value
        low_value = value.astype(bf16)
        d_branch[whole, :] = low_value
        sums[0:8, :] += eight(by_gain)
        sums[8:16, :] += eight(e)
        sums[16:24, :] += eight(widen(low_value))

    by_rows(mid.shape[0] // 2, norm)
    d_att[...] = mm_t(d_branch[...], w_proj[...]).astype(bf16)
    for h in range(heads):
        q, k, v = heads_of(qkv, width, size, h)
        d = d_att[:, h * size : (h + 1) * size]
        s = mm_t(q, k)
        e = jnp.exp(s - jnp.max(s, axis=-1, keepdims=True))
        p = e / jnp.sum(e, axis=-1, keepdims=True)
        dp = mm_t(d, v)
        ds = (p * (dp - jnp.sum(p * dp, axis=-1, keepdims=True))).astype(bf16)
        dq = (widen(mm(ds, k).astype(bf16)) * 0.125).astype(bf16)
        dk = t_mm(ds, q).astype(bf16)
        dv = t_mm(p.astype(bf16), d).astype(bf16)
        for i, value in enumerate((dq, dk, dv)):
            d_joined[:, i * width + h * size : i * width + (h + 1) * size] = value
    joined_sum[...] = eight(widen(d_joined[...]))
    by_cols(
        part.shape[1], lambda cols: put_part(part, low, cols, mm_t(d_joined[...], w_qkv[cols, :]))
    )


def attend_back(grad, mid, sent, vec, qkv, w_proj, w_qkv, heads, size):
    toks, width = mid.shape
    wide = 3 * heads * size
    outs = [((toks, width), f32), ((toks, width), bf16), ((toks, wide), bf16)]
    outs = outs + [((toks, width), f32), ((toks, width), bf16)]
    outs = outs + [((24, width), f32), ((8, wide), f32)]
    args = [grad, mid, *sent, vec, qkv, w_proj, w_qkv]
    flops = 8 * toks * width * heads * size + 10 * heads * toks * toks * size
    return call(
        functools.partial(attend_back_body, heads, size),
        outs,
        args,
        flops,
        heads * toks * toks,
        [pltpu.VMEM((toks, heads * size), bf16)],
    )


def last_body(base, d_mid, s0, s1, s2, s3, vec, grad, sums):
    sums[...] = jnp.zeros_like(sums)

    def norm(whole, half, part_rows):
        e = summed((s0, s1, s2, s3), whole, half, part_rows)
        d, by_gain = norm_grad(e, widen(base[whole, :]), vec[0:1, :])
        grad[whole, :] = d_mid[whole, :] + d
        sums[0:8, :] += eight(by_gain)
        sums[8:16, :] += eight(e)

    by_rows(base.shape[0] // 2, norm)


def last_back(base, d_mid, sent, vec):
    outs = [(base.shape, f32), ((16, base.shape[1]), f32)]
    return call(last_body, outs, [base, d_mid, *sent, vec], 20 * base.size)


def place_body(count, rows, extra, at_ref, *refs):
    blocks, outs, sems = refs[:count], refs[count:-1], refs[-1]
    copies = []
    for i in range(count):
        start = pl.multiple_of(at_ref[i] * rows, rows)
        source = blocks[i].at[pl.ds(0, rows)] if extra else blocks[i]
        copies.append(
            pltpu.make_async_copy(source, outs[0].at[pl.ds(start, rows)], sems.at[0, i])
        )
        if extra:
            start = pl.multiple_of(at_ref[i] * extra, extra)
            copies.append(
                pltpu.make_async_copy(
                    blocks[i].at[pl.ds(rows, extra)],
                    outs[1].at[pl.ds(start, extra)],
                    sems.at[1, i],
                )
            )
    for copy in copies:
        copy.start()
    for copy in copies:
        copy.wait()


def place(blocks, at, extra):
    count, (rows, cols) = len(blocks), blocks[0].shape
    outs = [jax.ShapeDtypeStruct((count * (rows - extra), cols), bf16)]
    if extra:
        outs.append(jax.ShapeDtypeStruct((count * extra, cols), bf16))
    return pl.pallas_call(
        functools.partial(place_body, count, rows - extra, extra),
        grid_spec=pltpu.PrefetchScalarGridSpec(
            num_scalar_prefetch=1,
            grid=(),
            in_specs=[pl.BlockSpec(memory_space=pltpu.VMEM)] * count,
            out_specs=[pl.BlockSpec(memory_space=pl.ANY)] * len(outs),
            scratch_shapes=[pltpu.SemaphoreType.DMA((2, count))],
        ),
        out_shape=tuple(outs),
        compiler_params=pltpu.CompilerParams(vmem_limit_bytes=VMEM_LIMIT),
        cost_estimate=pl.CostEstimate(
            flops=0, bytes_accessed=4 * count * rows * cols, transcendentals=0
        ),
        name="place",
    )(at, *blocks)


def gather_rows(unit, me, n, extra=0):
    nz = n // 2
    blocks = [unit] + [z_from(unit, k, n) for k in range(1, nz)]
    blocks = blocks + [x_swap(block, n) for block in blocks]
    z, x = me // 2, me % 2
    at = [((z + k) % nz) * 2 + x for k in range(nz)]
    at = at + [((z + k) % nz) * 2 + 1 - x for k in range(nz)]
    return place(blocks, jnp.stack(at).astype(jnp.int32), extra)


def gather_line(unit, me, n):
    nz = n // 2
    blocks = [unit] + [z_from(unit, k, n) for k in range(1, nz)]
    z = me // 2
    at = jnp.stack([(z + k) % nz for k in range(nz)]).astype(jnp.int32)
    return place(blocks, at, 0)[0]


def scatter_line(grad, me, n):
    nz = n // 2
    z = me // 2
    total = widen(pick(grad, 0, z))
    for k in range(1, nz):
        sent = pick(grad, 0, (z - k) % nz)
        came = z_from(sent, k, n)
        total = total + widen(came)
    return total


def scatter_rows(grad, me, n):
    nz = n // 2
    rows = grad.shape[0] // n
    blocks = grad.reshape(nz, 2, rows, grad.shape[1])
    x = me % 2
    sent = pick(blocks, 1, 1 - x)
    other = x_swap(sent, n)
    summed_low = (widen(pick(blocks, 1, x)) + widen(other)).astype(grad.dtype)
    return scatter_line(summed_low, me, n)


def send_part(part, low):
    side = core_swap(low)
    half = part.shape[0] // 2
    mine = (part[:half] + widen(side[half:])).astype(bf16)
    across = y_swap(mine)
    beside = core_swap(across)
    return part, side, across, beside


def on_device(
    clips_in,
    cotangent,
    clip_mask,
    norm1_gain,
    norm1_bias,
    qkv_weight,
    query_bias,
    value_bias,
    proj_weight,
    proj_bias,
    norm2_gain,
    norm2_bias,
    up_weight,
    up_bias,
    down_weight,
    down_bias,
    *,
    n,
):
    c, y, f = lax.axis_index("seq"), lax.axis_index("replica"), lax.axis_index("fsdp")
    quarter = 2 * y + c
    toks, width = clips_in.shape[1], clips_in.shape[2]
    rows = qkv_weight.shape[1]
    hid_rows = down_weight.shape[1]
    hidden = up_weight.shape[2]
    size = width // HEADS
    heads = HEADS // 4
    fast = n == 8 and rows == size and hid_rows == 4 * rows

    def pair_tokens(own):
        side = core_swap(own)
        across = y_swap(own)
        beside = core_swap(across)
        mine = jnp.concatenate([own, side], axis=0)
        other = jnp.concatenate([across, beside], axis=0)
        return jnp.where(y == 0, mine, other), jnp.where(y == 0, other, mine)

    def qkv_cols(w, at):
        w = w.reshape(*w.shape[:-1], 3, heads, 4, size)
        return pick(w, w.ndim - 2, at).reshape(*w.shape[:-4], 3 * heads * size)

    def up_cols(w, at_c, at_y):
        w = w.reshape(*w.shape[:-1], n, 2, 2, hid_rows // 2)
        w = pick(w, w.ndim - 2, at_y)
        return pick(w, w.ndim - 2, at_c).reshape(*w.shape[:-3], hidden // 4)

    def both(mine, theirs, axis):
        return jnp.where(
            c == 0,
            jnp.concatenate([mine, theirs], axis=axis),
            jnp.concatenate([theirs, mine], axis=axis),
        )

    flat = [
        norm1_gain,
        norm1_bias,
        query_bias,
        value_bias,
        proj_bias,
        norm2_gain,
        norm2_bias,
        down_bias,
    ]
    packed = jnp.concatenate(flat + [up_bias], axis=1)
    weights = []
    if fast:
        theirs = qkv_cols(qkv_weight, 2 * y + 1 - c)
        small = jnp.concatenate([packed, jnp.zeros((6, packed.shape[1]), bf16)], axis=0)
        theirs = jnp.concatenate([theirs.reshape(2 * rows, -1), small], axis=0)
        theirs = core_swap(theirs)
        mine = qkv_cols(qkv_weight, quarter)
        qkv_units = [
            both(mine[layer], theirs[layer * rows : (layer + 1) * rows], 0)
            for layer in range(LAYERS)
        ]
        side = theirs[2 * rows : 2 * rows + LAYERS]
        spare = jnp.zeros((16 - 2 * LAYERS, packed.shape[1]), bf16)
        qkv_units[0] = jnp.concatenate([qkv_units[0], both(packed, side, 0), spare], axis=0)
        up_units = both(up_cols(up_weight, c, y), core_swap(up_cols(up_weight, 1 - c, y)), 1)
        down_units = lax.dynamic_slice_in_dim(
            down_weight, y * (hid_rows // 2), hid_rows // 2, axis=1
        )
        proj_units = jnp.where(f % 2 == y, proj_weight, x_swap(proj_weight, n))
        everything = None
        for layer in range(LAYERS):
            extra = 16 if layer == 0 else 0
            got = gather_rows(qkv_units[layer], f, n, extra)
            if extra:
                everything = got[1].reshape(n, 16, -1)[:, : 2 * LAYERS]
                everything = everything.reshape(n, 2, LAYERS, -1).reshape(2 * n, LAYERS, -1)
            weights.append(
                (
                    got[0],
                    gather_line(proj_units[layer], f, n),
                    gather_rows(up_units[layer], f, n)[0],
                    gather_rows(down_units[layer], f, n)[0],
                )
            )
    else:
        everything = lax.all_gather(packed, ("fsdp", "seq"), axis=0)
        for layer in range(LAYERS):
            full = [
                lax.all_gather(w[layer], ("fsdp", "seq"), axis=0, tiled=True)
                for w in (qkv_weight, proj_weight, up_weight, down_weight)
            ]
            by_head = full[1].reshape(heads, 4, size, width)
            by_hid = full[3].reshape(n, 2, 2, hid_rows // 2, width)
            weights.append(
                (
                    qkv_cols(full[0], quarter),
                    pick(by_head, 1, quarter).reshape(heads * size, width),
                    up_cols(full[2], c, y),
                    pick(pick(by_hid, 2, y), 1, c).reshape(hidden // 4, width),
                )
            )

    smalls = []
    for layer in range(LAYERS):
        here = everything[:, layer]
        vectors = here[:, : 8 * rows].reshape(2 * n, 8, rows).transpose(1, 0, 2)
        vectors = widen(vectors.reshape(8, width))
        up_b = here[:, 8 * rows :].reshape(n, 2, 2, hid_rows // 2)
        up_b = widen(pick(pick(up_b, 2, y), 1, c).reshape(1, hidden // 4))
        by_head = vectors.reshape(8, heads, 4, size)
        by_head = pick(by_head, 2, quarter).reshape(8, heads * size)
        zero = jnp.zeros_like(by_head[0])
        add = jnp.concatenate([by_head[2], zero, by_head[3]])
        times = jnp.concatenate([zero + 0.125, zero + 1.0, zero + 1.0])
        smalls.append((vectors, jnp.stack([add, times]), up_b))

    streams = range(2)
    resid = list(pair_tokens(clips_in[0]))
    sent = [None, None]
    stash = []
    for layer in range(LAYERS):
        vectors, fix, up_b = smalls[layer]
        w_qkv, w_proj, w_up, w_down = weights[layer]
        past = smalls[layer - 1][0][7] if layer else vectors[7]
        vec_one = jnp.stack([vectors[0], vectors[1], past])
        vec_two = jnp.stack([vectors[5], vectors[6], vectors[4]])
        kept = []
        for s in streams:
            before, normed, qkv, attended, part, low = attend(
                resid[s], sent[s], vec_one, w_qkv, fix, w_proj, heads, size
            )
            got = send_part(part, low)
            mid, normed_two, active, slope = go_up(before, got, vec_two, w_up, up_b)
            kept.append((before, normed, qkv, attended, mid, normed_two, active, slope))
            part, low = go_down(active, w_down)
            sent[s] = send_part(part, low)
            resid[s] = mid
        stash.append(kept)

    def own_rows(pair):
        return jnp.where(y == 0, pair[0][:toks], pair[1][:toks])

    whole = [
        resid[s][:toks]
        + (
            (sent[s][0][:toks] + widen(sent[s][1][toks:])) + widen(sent[s][2])
            + smalls[-1][0][7]
        )
        for s in streams
    ]
    clips_out = own_rows(whole).astype(bf16)[None]

    masked = (widen(cotangent[0]) * widen(clip_mask)[0]).astype(bf16)
    start = pair_tokens(masked)
    grads = [None] * LAYERS
    mlp_sums = [None] * LAYERS
    att_sums = [None] * LAYERS
    d_mid, sent = [None, None], [None, None]

    def both_t_mm(left, right):
        return t_mm(
            jnp.concatenate(left, axis=0), jnp.concatenate(right, axis=0)
        ).astype(bf16)

    norm_one_sums = [None] * LAYERS
    for layer in reversed(range(LAYERS)):
        vectors = smalls[layer][0]
        w_qkv, w_proj, w_up, w_down = weights[layer]
        kept = stash[layer]
        d_mlp, d_pre, d_branch, d_joined, grad = [], [], [], [], []
        ups, sums = [], []
        last = layer == LAYERS - 1
        for s in streams:
            slope = kept[s][7]
            if last:
                got = mlp_back(start[s], None, None, None, None, slope, w_down, w_up)
                grad.append(start[s])
                d_mlp.append(start[s])
            else:
                after = stash[layer + 1][s][0]
                vec = smalls[layer + 1][0][0:1]
                got = mlp_back(None, after, d_mid[s], sent[s], vec, slope, w_down, w_up)
                grad.append(got[0])
                d_mlp.append(got[1])
                sums.append(got[6])
                got = got[2:6]
            d_pre.append(got[0])
            ups.append(got[3])
            sent[s] = send_part(got[1], got[2])
        if last:
            down_sum = sum(jnp.sum(widen(d), axis=0) for d in d_mlp)
        else:
            total = jnp.sum((sums[0] + sums[1]).reshape(3, 8, width), axis=1)
            norm_one_sums[layer + 1] = total[:2]
            down_sum = total[2]
        g_down = both_t_mm([k[6] for k in kept], d_mlp)
        g_up = both_t_mm([k[5] for k in kept], d_pre)
        mlp_sums[layer] = (down_sum, jnp.sum(ups[0] + ups[1], axis=0))
        sums, joined = [], []
        for s in streams:
            _, _, qkv, _, mid = kept[s][:5]
            got = attend_back(grad[s], mid, sent[s], vectors[5:6], qkv, w_proj, w_qkv, heads, size)
            d_mid[s] = got[0]
            d_branch.append(got[1])
            d_joined.append(got[2])
            sums.append(got[5])
            joined.append(got[6])
            sent[s] = send_part(got[3], got[4])
        g_proj = both_t_mm([k[3] for k in kept], d_branch)
        g_qkv = both_t_mm([k[1] for k in kept], d_joined)
        total = jnp.sum((sums[0] + sums[1]).reshape(3, 8, width), axis=1)
        att_sums[layer] = (total, jnp.sum(joined[0] + joined[1], axis=0))
        grads[layer] = (g_qkv, g_proj, g_up, g_down)
    final = [last_back(stash[0][s][0], d_mid[s], sent[s], smalls[0][0][0:1]) for s in streams]
    total = jnp.sum((final[0][1] + final[1][1]).reshape(2, 8, width), axis=1)
    norm_one_sums[0] = total
    input_grad = own_rows([final[0][0], final[1][0]])[None]

    here = (jnp.arange(4) == quarter).reshape(1, 1, 4, 1)
    at_c = (jnp.arange(2) == c).reshape(1, 2, 1, 1)
    at_y = (jnp.arange(2) == y).reshape(1, 1, 2, 1)
    by_owner = []
    for layer in range(LAYERS):
        att, joined = att_sums[layer]
        down_sum, up_sum = mlp_sums[layer]
        joined = joined.reshape(3, heads, 1, size)[0::2]
        joined = jnp.where(here, joined, 0.0).reshape(2, width)
        alike = [norm_one_sums[layer], att, down_sum[None]]
        alike = 0.25 * jnp.concatenate(alike, axis=0)
        vecs = jnp.concatenate([alike, joined], axis=0)
        vecs = vecs.reshape(8, 2 * n, rows).transpose(1, 0, 2).reshape(n, 2, 8 * rows)
        up = jnp.where(at_c & at_y, up_sum.reshape(n, 1, 1, hid_rows // 2), 0.0)
        by_owner.append(jnp.concatenate([vecs, up.reshape(n, 2, hid_rows)], axis=2))
    by_owner = jnp.stack(by_owner, axis=2)
    if fast:
        tiny = by_owner.reshape(n * 2 * LAYERS, -1)
        tiny = scatter_rows(tiny, f, n).reshape(2, LAYERS, -1)
        tiny = pick(tiny, 0, c) + core_swap(pick(tiny, 0, 1 - c))
        tiny = tiny + y_swap(tiny)
    else:
        total = lax.psum(by_owner, ("fsdp", "seq", "replica"))
        tiny = pick(pick(total, 0, f), 0, c)
    vec = tiny[:, : 8 * rows].reshape(LAYERS, 8, rows)
    up_bias_grad = tiny[:, 8 * rows :]

    def in_order(mine, theirs, first):
        return jnp.where(first == 0, mine, theirs), jnp.where(first == 0, theirs, mine)

    def to_rows(grad):
        halves = grad.reshape(2, rows, grad.shape[1])
        theirs = core_swap(pick(halves, 0, 1 - c).astype(bf16))
        pair = jnp.stack(in_order(pick(halves, 0, c), widen(theirs), c), axis=1)
        across = widen(y_swap(pair.astype(bf16)))
        return jnp.concatenate(in_order(pair, across, y), axis=1)

    outs = []
    for layer in range(LAYERS):
        g_qkv, g_proj, g_up, g_down = grads[layer]
        if fast:
            g = to_rows(scatter_rows(g_qkv, f, n))
            g = g.reshape(rows, 4, 3, heads, size).transpose(0, 2, 3, 1, 4)
            qkv_out = g.reshape(rows, 3 * width)
            g = scatter_line(g_proj.reshape(n // 2, rows, width), f, n)
            g = g + widen(x_swap(g.astype(bf16), n))
            proj_out = jnp.where(f % 2 == y, g, widen(y_swap(g.astype(bf16))))
            g = to_rows(scatter_rows(g_up, f, n))
            g = g.reshape(rows, 2, 2, n, hid_rows // 2).transpose(0, 3, 2, 1, 4)
            up_out = g.reshape(rows, hidden)
            g = scatter_rows(g_down, f, n)
            across = widen(y_swap(g.astype(bf16)))
            down_out = jnp.concatenate(in_order(g, across, y), axis=0)
        else:
            axes = ("replica", "seq")

            def owned(full):
                block = lax.psum_scatter(full, "fsdp", scatter_dimension=0, tiled=True)
                half = block.shape[0] // 2
                return widen(lax.dynamic_slice_in_dim(block, c * half, half, axis=0))

            g = lax.all_gather(g_qkv, axes, axis=0).reshape(4, width, 3, heads, size)
            qkv_out = owned(g.transpose(1, 2, 3, 0, 4).reshape(width, 3 * width))
            g = lax.all_gather(g_proj, axes, axis=0).reshape(4, heads, size, width)
            proj_out = owned(g.transpose(1, 0, 2, 3).reshape(width, width))
            g = lax.all_gather(g_up, axes, axis=0)
            g = g.reshape(2, 2, width, n, hid_rows // 2)
            up_out = owned(g.transpose(2, 3, 1, 0, 4).reshape(width, hidden))
            g = lax.all_gather(g_down, axes, axis=0)
            g = g.reshape(2, 2, n, hid_rows // 2, width)
            down_out = owned(g.transpose(2, 1, 0, 3, 4).reshape(hidden, width))
        outs.append((qkv_out, proj_out, up_out, down_out))
    qkv_out, proj_out, up_out, down_out = [
        jnp.stack([outs[layer][i] for layer in range(LAYERS)]) for i in range(4)
    ]
    return (
        clips_out,
        input_grad,
        vec[:, 0],
        vec[:, 1],
        qkv_out,
        vec[:, 6],
        vec[:, 7],
        proj_out,
        vec[:, 4],
        vec[:, 2],
        vec[:, 3],
        up_out,
        up_bias_grad,
        down_out,
        vec[:, 5],
    )


def solution(mesh):
    tokens = P(("fsdp", "replica"), "seq", None)
    vector = P(None, ("fsdp", "seq"))
    matrix = P(None, ("fsdp", "seq"), None)
    kinds = [
        vector,
        vector,
        matrix,
        vector,
        vector,
        matrix,
        vector,
        vector,
        vector,
        matrix,
        vector,
        matrix,
        vector,
    ]
    return jax.shard_map(
        functools.partial(on_device, n=mesh.shape["fsdp"]),
        mesh=mesh,
        in_specs=(tokens, tokens, P(("fsdp", "replica")), *kinds),
        out_specs=(tokens, tokens, *kinds),
        check_vma=False,
    )
```

```python
import functools

import jax
import jax.numpy as jnp
from jax import lax
from jax.experimental import pallas as pl
from jax.experimental.pallas import tpu as pltpu
from jax.sharding import PartitionSpec as P


HEADS = 16
LAYERS = 2
norm_eps = 1e-06
bf16 = jnp.bfloat16
f32 = jnp.float32


def widen(array):
    return array.astype(f32)


def dot(a, b, dims):
    return lax.dot_general(a, b, (dims, ((), ())), preferred_element_type=f32)


def mm(a, b):
    return dot(a, b, ((1,), (0,)))


def mm_t(a, b):
    return dot(a, b, ((1,), (1,)))


def t_mm(a, b):
    return dot(a, b, ((0,), (0,)))


PAIR = [(0, 1), (1, 0)]


def core_swap(v):
    return lax.ppermute(v, "seq", PAIR)


def y_swap(v):
    return lax.ppermute(v, "replica", PAIR)


def x_swap(v, n):
    return lax.ppermute(v, "fsdp", [(f, f ^ 1) for f in range(n)])


def z_from(v, k, n):
    nz = n // 2
    return lax.ppermute(
        v, "fsdp", [(((z + k) % nz) * 2 + x, z * 2 + x) for z in range(nz) for x in range(2)]
    )


def pick(array, axis, at):
    return lax.dynamic_index_in_dim(array, at, axis, keepdims=False)


TILE = 32
COLS = 256
VMEM_LIMIT = 20 * 1024 * 1024
HBM = pltpu.MemorySpace.HBM


def call(body, outs, args, flops, transcendentals=0, scratch=(), smem=0):
    shapes = tuple(jax.ShapeDtypeStruct(o[0], o[1]) for o in outs)
    far = [i for i, o in enumerate(outs) if len(o) > 2 and o[2]]
    n_in, n_out, n_far = len(args), len(outs), len(far)

    def run(*refs):
        out_refs = list(refs[n_in : n_in + n_out])
        rest = refs[n_in + n_out :]
        sems = rest[-1] if far else None
        copies = {}
        for j, i in enumerate(far):
            copies[i] = pltpu.make_async_copy(rest[j], out_refs[i], sems.at[j])
            out_refs[i] = rest[j]
        extra = rest[n_far:-1] if far else rest[n_far:]
        body(lambda i: copies[i].start(), *refs[:n_in], *out_refs, *extra)
        for copy in copies.values():
            copy.wait()

    touched = sum(a.size * a.dtype.itemsize for a in (*args, *shapes))
    scratch = [pltpu.VMEM(*outs[i][:2]) for i in far] + list(scratch)
    if far:
        scratch.append(pltpu.SemaphoreType.DMA((n_far,)))
    spaces = [pltpu.SMEM if i < smem else pltpu.VMEM for i in range(n_in)]
    return pl.pallas_call(
        run,
        out_shape=shapes,
        in_specs=[pl.BlockSpec(memory_space=s) for s in spaces],
        out_specs=tuple(
            pl.BlockSpec(memory_space=HBM if i in far else pltpu.VMEM) for i in range(n_out)
        ),
        scratch_shapes=scratch,
        compiler_params=pltpu.CompilerParams(vmem_limit_bytes=VMEM_LIMIT),
        cost_estimate=pl.CostEstimate(
            flops=flops, bytes_accessed=touched, transcendentals=transcendentals
        ),
    )(*args)


def norm_parts(inputs):
    center = inputs - jnp.mean(inputs, axis=-1, keepdims=True)
    spread = jnp.mean(center * center, axis=-1, keepdims=True)
    scale = lax.rsqrt(spread + norm_eps)
    return center * scale, scale


def norm_grad(e, inputs, gain):
    unit, scale = norm_parts(inputs)
    eg = e * gain
    d = scale * (
        eg
        - jnp.mean(eg, axis=-1, keepdims=True)
        - unit * jnp.mean(eg * unit, axis=-1, keepdims=True)
    )
    return d, e * unit


def eight(v):
    return jnp.sum(v.reshape(v.shape[0] // 8, 8, v.shape[1]), axis=0)


def one(v):
    return jnp.sum(v, axis=0, keepdims=True)


def by_rows(half_rows, step):
    for half in range(2):

        @pl.loop(0, half_rows // TILE)
        def _(i):
            start = pl.multiple_of(i * TILE, TILE)
            step(pl.ds(half * half_rows + start, TILE), half, pl.ds(start, TILE))


def by_cols(width, step):
    @pl.loop(0, width // COLS)
    def _(i):
        step(pl.ds(pl.multiple_of(i * COLS, COLS), COLS))


def summed(sent, whole, half, part):
    rows = sent[1].shape[0] // 2
    side = pl.ds((1 - half) * rows + part.start, TILE)
    total = widen(sent[0][whole, :]) + widen(sent[1][side, :])
    return total + widen(sent[2 + half][part, :])


def put(ref, cols, value):
    ref[:, cols] = value.astype(ref.dtype)


def heads_of(ref, width, size, h):
    return [ref[:, i * width + h * size : i * width + (h + 1) * size] for i in range(3)]


GAIN_ONE, SHIFT_ONE, QUERY_B, VALUE_B, PROJ_B, GAIN_TWO, SHIFT_TWO, DOWN_B = range(8)


def row(vec, which, layer):
    at = 2 * which + layer
    return vec[at : at + 1, :]


def attend_body(layer, heads, size, flush, *refs):
    if layer == 0:
        base, vec, w_qkv, fix, w_proj, normed, qkv, attended, stat, low = refs
        sent, shift = None, 0
    else:
        base, s0, s1, s2, s3, vec, w_qkv, fix, w_proj = refs[:9]
        resid, normed, qkv, attended, stat, low = refs[9:]
        sent, shift = (s0, s1, s2, s3), 1
    width = heads * size

    def norm(whole, half, part_rows):
        value = widen(base[whole, :])
        if sent is not None:
            value = value + (summed(sent, whole, half, part_rows) + row(vec, DOWN_B, layer - 1))
            resid[whole, :] = value
        unit, _ = norm_parts(value)
        normed[whole, :] = (
            unit * row(vec, GAIN_ONE, layer) + row(vec, SHIFT_ONE, layer)
        ).astype(bf16)

    by_rows(base.shape[0] // 2, norm)
    for i in range(shift + 1):
        flush(i)

    def project(cols):
        value = mm(normed[...], w_qkv[:, cols]) + fix[2 * layer : 2 * layer + 1, cols]
        qkv[:, cols] = (value * fix[2 * layer + 1 : 2 * layer + 2, cols]).astype(bf16)

    by_cols(3 * width, project)
    flush(shift + 1)
    for h in range(heads):
        q, k, v = heads_of(qkv, width, size, h)
        s = mm_t(q, k)
        peak = jnp.max(s, axis=-1, keepdims=True)
        e = jnp.exp(s - peak)
        total = jnp.sum(e, axis=-1, keepdims=True)
        value = mm(e.astype(bf16), v) * (1.0 / total)
        attended[:, h * size : (h + 1) * size] = value.astype(bf16)
        stat[:, h : h + 1] = peak + jnp.log(total)
    flush(shift + 2)
    flush(shift + 3)
    by_cols(low.shape[1], lambda cols: put(low, cols, mm(attended[...], w_proj[:, cols])))


def attend(base, sent, vec, w_qkv, fix, w_proj, layer, heads, size):
    toks, width = base.shape
    outs = [((toks, width), bf16, True), ((toks, 3 * heads * size), bf16, True)]
    outs = outs + [((toks, heads * size), bf16, True), ((toks, 128), f32, True)]
    outs = outs + [((toks, width), bf16)]
    if layer:
        outs = [((toks, width), f32, True)] + outs
    args = [base, *(sent or ()), vec, w_qkv, fix, w_proj]
    flops = 8 * toks * width * heads * size + 4 * heads * toks * toks * size
    body = functools.partial(attend_body, layer, heads, size)
    got = call(body, outs, args, flops, heads * toks * toks)
    return got if layer else (base, *got)


ROOT_HALF = 0.7071067811865476
ROOT_TWO_PI_INV = 0.3989422804014327


def up_body(layer, flush, base, s0, s1, s2, s3, vec, w_up, up_b, mid, normed, active, slope):
    def norm(whole, half, part_rows):
        value = widen(base[whole, :])
        value = value + (
            summed((s0, s1, s2, s3), whole, half, part_rows) + row(vec, PROJ_B, layer)
        )
        mid[whole, :] = value
        unit, _ = norm_parts(value)
        normed[whole, :] = (
            unit * row(vec, GAIN_TWO, layer) + row(vec, SHIFT_TWO, layer)
        ).astype(bf16)

    by_rows(base.shape[0] // 2, norm)
    flush(0)
    flush(1)

    def up(cols):
        pre = mm(normed[...], w_up[:, cols]) + up_b[layer : layer + 1, cols]
        half = 0.5 * (1.0 + lax.erf(pre * ROOT_HALF))
        put(active, cols, pre * half)
        put(slope, cols, half + pre * (ROOT_TWO_PI_INV * jnp.exp(-0.5 * pre * pre)))

    by_cols(w_up.shape[1], up)
    flush(2)
    flush(3)


def go_up(base, sent, vec, w_up, up_b, layer):
    toks, width = base.shape
    hid = w_up.shape[1]
    outs = [((toks, width), f32, True), ((toks, width), bf16, True)]
    outs = outs + [((toks, hid), bf16, True), ((toks, hid), bf16, True)]
    args = [base, *sent, vec, w_up, up_b]
    body = functools.partial(up_body, layer)
    return call(body, outs, args, 2 * toks * width * hid, toks * hid)


def down_body(flush, active, w_down, low):
    by_cols(low.shape[1], lambda cols: put(low, cols, mm(active[...], w_down[:, cols])))


def go_down(active, w_down):
    outs = [((active.shape[0], w_down.shape[1]), bf16)]
    flops = 2 * active.size * w_down.shape[1]
    return call(down_body, outs, [active, w_down], flops)[0]


def mlp_back_tail(flush, at, d_mlp, slope, w_down, w_up, d_pre, low, up_sum):
    def back(cols):
        value = (mm_t(d_mlp[...], w_down[cols, :]) * widen(slope[:, cols])).astype(bf16)
        d_pre[:, cols] = value
        up_sum[:, cols] = eight(widen(value))

    by_cols(w_down.shape[0], back)
    flush(at)
    by_cols(low.shape[1], lambda cols: put(low, cols, mm_t(d_pre[...], w_up[cols, :])))


def mlp_back_first(flush, d_mlp, slope, w_down, w_up, d_pre, low, up_sum, sums):
    sums[...] = jnp.zeros_like(sums)

    def count(whole, half, part_rows):
        sums[16:24, :] += eight(widen(d_mlp[whole, :]))

    by_rows(d_mlp.shape[0] // 2, count)
    mlp_back_tail(flush, 0, d_mlp, slope, w_down, w_up, d_pre, low, up_sum)


def mlp_back_body(layer, flush, base, d_mid, s0, s1, s2, s3, vec, slope, w_down, w_up, *outs):
    grad, d_mlp, d_pre, low, up_sum, sums = outs
    sums[...] = jnp.zeros_like(sums)

    def norm(whole, half, part_rows):
        e = summed((s0, s1, s2, s3), whole, half, part_rows)
        d, by_gain = norm_grad(e, widen(base[whole, :]), row(vec, GAIN_ONE, layer + 1))
        value = d_mid[whole, :] + d
        grad[whole, :] = value
        low_value = value.astype(bf16)
        d_mlp[whole, :] = low_value
        sums[0:8, :] += eight(by_gain)
        sums[8:16, :] += eight(e)
        sums[16:24, :] += eight(widen(low_value))

    by_rows(base.shape[0] // 2, norm)
    flush(0)
    flush(1)
    mlp_back_tail(flush, 2, d_mlp, slope, w_down, w_up, d_pre, low, up_sum)


def mlp_back(first, base, d_mid, sent, vec, slope, w_down, w_up, layer):
    toks, hid = slope.shape
    width = w_up.shape[0]
    outs = [((toks, hid), bf16, True), ((toks, width), bf16), ((8, hid), f32), ((24, width), f32)]
    flops = 4 * toks * hid * width
    if first is not None:
        return call(mlp_back_first, outs, [first, slope, w_down, w_up], flops)
    outs = [((toks, width), f32, True), ((toks, width), bf16, True), *outs]
    args = [base, d_mid, *sent, vec, slope, w_down, w_up]
    return call(functools.partial(mlp_back_body, layer), outs, args, flops)


def attend_back_body(layer, heads, size, flush, *refs):
    grad, mid, s0, s1, s2, s3, vec, qkv, stat, w_proj, w_qkv = refs[:11]
    d_mid, d_branch, d_joined, low, sums, joined_sum, d_att = refs[11:]
    width = heads * size
    sums[...] = jnp.zeros_like(sums)

    def norm(whole, half, part_rows):
        e = summed((s0, s1, s2, s3), whole, half, part_rows)
        d, by_gain = norm_grad(e, mid[whole, :], row(vec, GAIN_TWO, layer))
        value = widen(grad[whole, :]) + d
        d_mid[whole, :] = value
        low_value = value.astype(bf16)
        d_branch[whole, :] = low_value
        sums[0:8, :] += eight(by_gain)
        sums[8:16, :] += eight(e)
        sums[16:24, :] += eight(widen(low_value))

    by_rows(mid.shape[0] // 2, norm)
    flush(0)
    flush(1)
    d_att[...] = mm_t(d_branch[...], w_proj[...]).astype(bf16)
    rows = stat[...].T
    for h in range(heads):
        q, k, v = heads_of(qkv, width, size, h)
        d = d_att[:, h * size : (h + 1) * size]
        p = jnp.exp(mm_t(k, q) - rows[h : h + 1, :])
        dv = mm(p.astype(bf16), d)
        d_p = mm_t(v, d)
        ds = (p * (d_p - jnp.sum(p * d_p, axis=0, keepdims=True))).astype(bf16)
        dk = mm(ds, q)
        dq = widen(t_mm(ds, k).astype(bf16)) * 0.125
        for i, value in enumerate((dq, dk, dv)):
            at = i * width + h * size
            d_joined[:, at : at + size] = value.astype(bf16)
    flush(2)
    joined_sum[...] = eight(widen(d_joined[...]))
    by_cols(low.shape[1], lambda cols: put(low, cols, mm_t(d_joined[...], w_qkv[cols, :])))


def attend_back(grad, mid, sent, vec, qkv, stat, w_proj, w_qkv, layer, heads, size):
    toks, width = mid.shape
    wide = 3 * heads * size
    outs = [((toks, width), f32, True), ((toks, width), bf16, True), ((toks, wide), bf16, True)]
    outs = outs + [((toks, width), bf16), ((24, width), f32), ((8, wide), f32)]
    args = [grad, mid, *sent, vec, qkv, stat, w_proj, w_qkv]
    flops = 8 * toks * width * heads * size + 10 * heads * toks * toks * size
    return call(
        functools.partial(attend_back_body, layer, heads, size),
        outs,
        args,
        flops,
        heads * toks * toks,
        [pltpu.VMEM((toks, heads * size), bf16)],
    )


def last_body(flush, where, *refs):
    streams, vec, grad, sums = (refs[0:6], refs[6:12]), refs[12], refs[13], refs[14]
    sums[...] = jnp.zeros_like(sums)
    for s, (base, d_mid, *sent) in enumerate(streams):

        def norm(whole, half, part_rows):
            e = summed(sent, whole, half, part_rows)
            d, by_gain = norm_grad(e, widen(base[whole, :]), row(vec, GAIN_ONE, 0))
            sums[0:8, :] += eight(by_gain)
            sums[8:16, :] += eight(e)
            if half == 0:

                @pl.when(where[1] == s)
                def _():
                    grad[part_rows, :] = d_mid[whole, :] + d

        by_rows(base.shape[0] // 2, norm)
    flush(0)


def last_back(where, streams, vec):
    toks, width = streams[0][0].shape
    outs = [((toks // 2, width), f32, True), ((16, width), f32)]
    args = [where, *streams[0], *streams[1], vec]
    return call(last_body, outs, args, 20 * toks * width, smem=1)


def pick_body(toks, flush, where, own, side, across, beside, *outs):
    for i in range(2):
        at = slice(i * toks, (i + 1) * toks)
        for s in range(2):
            out = outs[2 * i + s]

            @pl.when(where[1] == s)
            def _():
                out[0:toks, :] = own[at, :]
                out[toks:, :] = side[at, :]

            @pl.when(where[1] != s)
            def _():
                out[0:toks, :] = across[at, :]
                out[toks:, :] = beside[at, :]

            flush(2 * i + s)


def halves(first, second, c):
    low = lax.broadcasted_iota(jnp.int32, first.shape, 1) < first.shape[1] // 2
    half = first.shape[1] // 2
    zero = jnp.where(low, first, pltpu.roll(second, half, 1))
    other = jnp.where(low, pltpu.roll(first, half, 1), second)
    return jnp.where(c == 0, zero, other), jnp.where(c == 0, other, zero)


def units_body(rows, heads, size, flush, where, qkv, up, down, small, *outs):
    q_mine, q_theirs, u_mine, u_theirs, d_unit = outs
    c, y = where[0], where[1]
    pair = 2 * size
    for layer in range(LAYERS):
        at = slice(layer * rows, (layer + 1) * rows)
        for t in range(3):
            for h in range(0, heads, 2):
                start = (t * heads + h) * 2 * pair
                tiles = [
                    widen(qkv[layer, :, pl.ds(pl.multiple_of(start + i * 2 * pair + y * pair, pair), pair)])
                    for i in range(2)
                ]
                mine, theirs = halves(*tiles, c)
                cols = slice((t * heads + h) * size, (t * heads + h + 2) * size)
                q_mine[at, cols] = mine.astype(bf16)
                q_theirs[at, cols] = theirs.astype(bf16)
        blocks = up.shape[2] // (4 * pair)
        for f in range(blocks):
            for ref, core in ((u_mine, c), (u_theirs, 1 - c)):
                start = pl.multiple_of(f * 4 * pair + core * 2 * pair + y * pair, pair)
                ref[at, f * pair : (f + 1) * pair] = up[layer, :, pl.ds(start, pair)]
        half = down.shape[1] // 2
        d_unit[layer] = down[layer, pl.ds(pl.multiple_of(y * half, half), half), :]
    q_theirs[2 * rows :, :] = jnp.zeros((16, q_theirs.shape[1]), bf16)
    q_theirs[2 * rows :, 0:pair] = small[...]


def join_body(rows, flush, where, q_mine, q_side, u_mine, u_side, small, up_b, p_own, p_side, *outs):
    q0, q1, u0, u1, p0, p1 = outs
    c, y, x = where[0], where[1], where[2]
    pair = small.shape[1]
    here = pl.ds(pl.multiple_of(c * rows, rows), rows)
    there = pl.ds(pl.multiple_of((1 - c) * rows, rows), rows)
    for layer, (q, u, p) in enumerate(((q0, u0, p0), (q1, u1, p1))):
        at = slice(layer * rows, (layer + 1) * rows)
        q[here, :] = q_mine[at, :]
        q[there, :] = q_side[at, :]
        u[here, :] = u_mine[at, :]
        u[there, :] = u_side[at, :]

        @pl.when(x == y)
        def _():
            p[...] = p_own[layer]

        @pl.when(x != y)
        def _():
            p[...] = p_side[layer]

    low = lax.broadcasted_iota(jnp.int32, small.shape, 1) < pair // 2
    own, side = widen(small[...]), widen(q_side[2 * rows :, 0:pair])
    both = jnp.where(c == 0, jnp.where(low, own, side), jnp.where(low, side, own))
    q0[2 * rows :, :] = jnp.zeros((16, q0.shape[1]), bf16)
    q0[2 * rows :, 0:pair] = both.astype(bf16)
    ups = widen(up_b[...])
    ups = jnp.where(y == 0, ups[:, 0:pair], ups[:, pair : 2 * pair])
    q0[2 * rows :, pair : 2 * pair] = ups.astype(bf16)


def prep_body(n, heads, size, flush, where, small, vec, fix, up_b):
    c, y = where[0], where[1]
    pair = 2 * size
    for f in range(n):
        vec[:, f * pair : (f + 1) * pair] = widen(small[:, f * 2 * pair : f * 2 * pair + pair])
        up_b[:, f * pair : (f + 1) * pair] = widen(
            small[:, f * 2 * pair + pair : (f + 1) * 2 * pair]
        )
    width = heads * size
    for layer in range(LAYERS):
        for t, which in ((0, QUERY_B), (2, VALUE_B)):
            for i in range(0, heads, 2):
                tiles = [
                    widen(small[:, pl.ds(pl.multiple_of((2 * (i + j) + y) * 2 * pair, 2 * pair), pair)])
                    for j in range(2)
                ]
                mine, _ = halves(*tiles, c)
                at = 2 * which + layer
                start = t * width + i * size
                fix[2 * layer : 2 * layer + 1, start : start + pair] = mine[at : at + 1, :]
        fix[2 * layer : 2 * layer + 1, width : 2 * width] = jnp.zeros((1, width), f32)
        fix[2 * layer + 1 : 2 * layer + 2, 0:width] = jnp.full((1, width), 0.125, f32)
        fix[2 * layer + 1 : 2 * layer + 2, width:] = jnp.ones((1, 2 * width), f32)


def place_body(count, rows, extra, at_ref, *refs):
    n_out = 2 if extra else 1
    blocks, outs, sems = refs[: -1 - n_out], refs[-1 - n_out : -1], refs[-1]
    copies = []
    per = count // len(blocks)
    for i in range(count):
        source, base = blocks[i // per], (i % per) * (rows + extra)
        start = pl.multiple_of(at_ref[i] * rows, rows)
        copies.append(
            pltpu.make_async_copy(
                source.at[pl.ds(base, rows)], outs[0].at[pl.ds(start, rows)], sems.at[0, i]
            )
        )
        if extra:
            start = pl.multiple_of(at_ref[i] * 256, 256)
            copies.append(
                pltpu.make_async_copy(
                    source.at[pl.ds(base + rows, extra), pl.ds(0, 256)],
                    outs[1].at[:, pl.ds(start, 256)],
                    sems.at[1, i],
                )
            )
    for copy in copies:
        copy.start()
    for copy in copies:
        copy.wait()


def place(blocks, at, count, extra):
    total, cols = sum(b.shape[0] for b in blocks), blocks[0].shape[1]
    rows = total // count - extra
    outs = [jax.ShapeDtypeStruct((count * rows, cols), bf16)]
    if extra:
        outs.append(jax.ShapeDtypeStruct((extra, count * 256), bf16))
    return pl.pallas_call(
        functools.partial(place_body, count, rows, extra),
        in_specs=[pl.BlockSpec(memory_space=pltpu.SMEM)]
        + [pl.BlockSpec(memory_space=pltpu.VMEM)] * len(blocks),
        out_specs=tuple([pl.BlockSpec(memory_space=pl.ANY)] * len(outs)),
        scratch_shapes=[pltpu.SemaphoreType.DMA((2, count))],
        out_shape=tuple(outs),
        compiler_params=pltpu.CompilerParams(vmem_limit_bytes=VMEM_LIMIT),
        cost_estimate=pl.CostEstimate(flops=0, bytes_accessed=4 * total * cols, transcendentals=0),
        name="place",
    )(at, *blocks)


def gather_rows(unit, me, n, extra=0):
    nz = n // 2
    line = [unit] + [z_from(unit, k, n) for k in range(1, nz)]
    line = jnp.concatenate(line, axis=0)
    other = x_swap(line, n)
    z, x = me // 2, me % 2
    at = [((z + k) % nz) * 2 + x for k in range(nz)]
    at = at + [((z + k) % nz) * 2 + 1 - x for k in range(nz)]
    return place([line, other], jnp.stack(at).astype(jnp.int32), n, extra)


def gather_line(unit, me, n):
    nz = n // 2
    blocks = [unit] + [z_from(unit, k, n) for k in range(1, nz)]
    z = me // 2
    at = jnp.stack([(z + k) % nz for k in range(nz)]).astype(jnp.int32)
    return place(blocks, at, nz, 0)[0]


def split_body(nz, flush, where, *refs):
    grad, other = (refs[0], refs[1]) if len(refs) == 2 + nz else (refs[0], None)
    outs = refs[-nz:]
    x, z = where[2], where[3]
    rows = outs[0].shape[0]
    for k in range(nz):
        to = lax.rem(z - k + nz, nz)
        if other is None:
            value = grad[pl.ds(pl.multiple_of(to * rows, rows), rows), :]
        else:
            mine = grad[pl.ds(pl.multiple_of((to * 2 + x) * rows, rows), rows), :]
            value = widen(mine) + widen(other[pl.ds(pl.multiple_of(to * rows, rows), rows), :])
        outs[k][...] = value.astype(outs[k].dtype)


def scatter(grad, where, me, n, line=False):
    nz = n // 2
    count = nz if line else n
    rows, cols = grad.shape[0] // count, grad.shape[1]
    args = [where, grad]
    if not line:
        blocks = grad.reshape(nz, 2, rows, cols)
        sent = pick(blocks, 1, 1 - me % 2).reshape(nz * rows, cols)
        args.append(x_swap(sent, n))
    outs = [((rows, cols), f32)] + [((rows, cols), grad.dtype)] * (nz - 1)
    got = call(functools.partial(split_body, nz), outs, args, grad.size, smem=1)
    return [got[0]] + [z_from(got[k], k, n) for k in range(1, nz)]


def total_of(refs):
    total = widen(refs[0][...])
    for ref in refs[1:]:
        total = total + widen(ref[...])
    return total


def rows_body(rows, flush, where, *refs):
    mine, sent, total = refs[-3:]
    total[...] = total_of(refs[:-3])
    c = where[0]
    mine[...] = total[pl.ds(pl.multiple_of(c * rows, rows), rows), :]
    sent[0:rows, :] = mine[...].astype(bf16)
    other = total[pl.ds(pl.multiple_of((1 - c) * rows, rows), rows), :]
    sent[rows:, :] = other.astype(bf16)


def to_rows(pieces, where):
    rows, cols = pieces[0].shape[0] // 2, pieces[0].shape[1]
    outs = [((rows, cols), f32), ((2 * rows, cols), bf16)]
    mine, sent = call(
        functools.partial(rows_body, rows),
        outs,
        [where, *pieces],
        4 * sent_size(pieces),
        scratch=[pltpu.VMEM((2 * rows, cols), f32)],
        smem=1,
    )
    across = y_swap(sent)
    side = core_swap(sent[rows:])
    beyond = core_swap(across[rows:])
    return mine, side, across, beyond


def sent_size(pieces):
    return sum(p.size for p in pieces)


def sum_body(flush, *refs):
    total = total_of(refs[:-2])
    refs[-2][...] = total
    refs[-1][...] = total.astype(refs[-1].dtype)


def both_types(pieces):
    shape = pieces[0].shape
    return call(sum_body, [(shape, f32), (shape, bf16)], list(pieces), sent_size(pieces))


def finish_body(layer, n, heads, size, first, where, *refs):
    q, u = refs[0:4], refs[4:8]
    d_own, d_side, p_own, p_side = refs[8:12]
    outs = refs[12 if first else 16 :][:4]
    b_q, b_p, b_u, b_d, sems = refs[-5:]
    c, y, x = where[0], where[1], where[2]
    pair = 2 * size
    rows = q[0].shape[0]

    def quarters(pieces, cols):
        mine, side = pieces[0][:, cols], widen(pieces[1][:, cols])
        across, beyond = widen(pieces[2][0:rows, cols]), widen(pieces[3][:, cols])
        here = (jnp.where(c == 0, mine, side), jnp.where(c == 0, side, mine))
        there = (jnp.where(c == 0, across, beyond), jnp.where(c == 0, beyond, across))
        return [
            [jnp.where(y == at, here[core], there[core]) for core in range(2)] for at in range(2)
        ]

    def out(i, buffer):
        return pltpu.make_async_copy(buffer, outs[i].at[layer], sems.at[i])

    for t in range(3):
        for h in range(0, heads, 2):
            at = (t * heads + h) * size
            got = quarters(q, slice(at, at + pair))
            for across in range(2):
                one_head, next_head = halves(*got[across], 0)
                start = (t * heads + h) * 2 * pair + across * pair
                b_q[:, start : start + pair] = one_head
                b_q[:, start + 2 * pair : start + 3 * pair] = next_head
    out(0, b_q).start()
    for f in range(n):
        got = quarters(u, slice(f * pair, (f + 1) * pair))
        for across in range(2):
            for core in range(2):
                start = f * 4 * pair + core * 2 * pair + across * pair
                b_u[:, start : start + pair] = got[across][core]
    out(2, b_u).start()
    half = d_own.shape[0]
    b_d[pl.ds(pl.multiple_of(y * half, half), half), :] = d_own[...]
    b_d[pl.ds(pl.multiple_of((1 - y) * half, half), half), :] = widen(d_side[...])
    out(3, b_d).start()
    b_p[...] = jnp.where(x == y, p_own[...], widen(p_side[...]))
    out(1, b_p).start()
    for i, buffer in enumerate((b_q, b_p, b_u, b_d)):
        out(i, buffer).wait()


def finish(where, q, u, d, p, past, layer, n, heads, size):
    rows = q[0].shape[0]
    width = HEADS * size
    hid = n * 8 * size
    shapes = [(rows, 3 * width), (rows, width), (rows, hid), (2 * d[0].shape[0], width)]
    args = [where, *q, *u, *d, *p]
    aliases = {}
    if past is not None:
        aliases = {len(args) + i: i for i in range(4)}
        args = args + list(past)
    first = past is None
    spaces = [pltpu.SMEM] + [pltpu.VMEM] * 12 + [HBM] * (0 if first else 4)
    return pl.pallas_call(
        functools.partial(finish_body, layer, n, heads, size, first),
        out_shape=tuple(jax.ShapeDtypeStruct((LAYERS, *s), f32) for s in shapes),
        in_specs=[pl.BlockSpec(memory_space=s) for s in spaces],
        out_specs=tuple([pl.BlockSpec(memory_space=HBM)] * 4),
        scratch_shapes=[pltpu.VMEM(s, f32) for s in shapes]
        + [pltpu.SemaphoreType.DMA((4,))],
        input_output_aliases=aliases,
        compiler_params=pltpu.CompilerParams(vmem_limit_bytes=VMEM_LIMIT),
        cost_estimate=pl.CostEstimate(
            flops=0, bytes_accessed=4 << 20, transcendentals=0
        ),
        name="finish",
    )(*args)


def pack_body(n, heads, size, flush, where, *refs):
    first, upper, lower, out = refs[0], refs[1:9], refs[9:17], refs[17]
    c, y = where[0], where[1]
    pair = 2 * size
    out[...] = jnp.zeros_like(out)

    def rows_of(ref, i):
        return one(ref[8 * i : 8 * i + 8, :])

    def put_vector(which, layer, value):
        at = 2 * which + layer
        for f in range(n):
            out[f, at : at + 1, :] = 0.25 * value[:, f * pair : (f + 1) * pair]

    def both(refs_of, i):
        return rows_of(refs_of[0], i) + rows_of(refs_of[1], i)

    for layer, group in ((1, upper), (0, lower)):
        ups, mlp, att, joined = group[0:2], group[2:4], group[4:6], group[6:8]
        put_vector(DOWN_B, layer, both(mlp, 2))
        put_vector(GAIN_TWO, layer, both(att, 0))
        put_vector(SHIFT_TWO, layer, both(att, 1))
        put_vector(PROJ_B, layer, both(att, 2))
        value = one(ups[0][...]) + one(ups[1][...])
        at = 16 + 4 * layer + 2 * c + y
        for f in range(n):
            out[f, pl.ds(at, 1), :] = value[:, f * pair : (f + 1) * pair]
        value = one(joined[0][...]) + one(joined[1][...])
        low = lax.broadcasted_iota(jnp.int32, (1, pair), 1) < size
        for t, which in ((0, QUERY_B), (2, VALUE_B)):
            at = 2 * which + layer
            for i in range(0, heads, 2):
                start = (t * heads + i) * size
                tile = value[:, start : start + pair]
                turned = pltpu.roll(jnp.broadcast_to(tile, (8, pair)), size, 1)[0:1, :]
                zero = jnp.zeros_like(tile)
                even = jnp.where(c == 0, jnp.where(low, tile, zero), jnp.where(low, zero, turned))
                odd = jnp.where(c == 0, jnp.where(low, turned, zero), jnp.where(low, zero, tile))
                out[2 * i + y, at : at + 1, :] = even
                out[2 * (i + 1) + y, at : at + 1, :] = odd
    mlp = lower[2:4]
    put_vector(GAIN_ONE, 1, both(mlp, 0))
    put_vector(SHIFT_ONE, 1, both(mlp, 1))
    put_vector(GAIN_ONE, 0, rows_of(first, 0))
    put_vector(SHIFT_ONE, 0, rows_of(first, 1))


def send_part(low):
    side = core_swap(low)
    half = low.shape[0] // 2
    mine = (widen(low[:half]) + widen(side[half:])).astype(bf16)
    across = y_swap(mine)
    beside = core_swap(across)
    return low, side, across, beside


def on_device(
    clips_in,
    cotangent,
    clip_mask,
    norm1_gain,
    norm1_bias,
    qkv_weight,
    query_bias,
    value_bias,
    proj_weight,
    proj_bias,
    norm2_gain,
    norm2_bias,
    up_weight,
    up_bias,
    down_weight,
    down_bias,
    *,
    n,
):
    c, y, f = lax.axis_index("seq"), lax.axis_index("replica"), lax.axis_index("fsdp")
    quarter = 2 * y + c
    toks, width = clips_in.shape[1], clips_in.shape[2]
    rows = qkv_weight.shape[1]
    hid_rows = down_weight.shape[1]
    hidden = up_weight.shape[2]
    size = width // HEADS
    heads = HEADS // 4
    fast = n == 8 and rows == size and hid_rows == 4 * rows

    where = jnp.stack([c, y, f % 2, f // 2]).astype(jnp.int32)

    masked = (widen(cotangent[0]) * widen(clip_mask)[0]).astype(bf16)
    own = jnp.concatenate([clips_in[0], masked], axis=0)
    side = core_swap(own)
    across = y_swap(own)
    beside = core_swap(across)
    got = call(
        functools.partial(pick_body, toks),
        [((2 * toks, width), bf16, True)] * 4,
        [where, own, side, across, beside],
        0,
        smem=1,
    )
    resid, start = list(got[:2]), got[2:]

    def qkv_cols(w, at):
        w = w.reshape(*w.shape[:-1], 3, heads, 4, size)
        return pick(w, w.ndim - 2, at).reshape(*w.shape[:-4], 3 * heads * size)

    def up_cols(w, at_c, at_y):
        w = w.reshape(*w.shape[:-1], n, 2, 2, hid_rows // 2)
        w = pick(w, w.ndim - 2, at_y)
        return pick(w, w.ndim - 2, at_c).reshape(*w.shape[:-3], hidden // 4)

    flat = [
        norm1_gain,
        norm1_bias,
        query_bias,
        value_bias,
        proj_bias,
        norm2_gain,
        norm2_bias,
        down_bias,
    ]
    weights = []
    if fast:
        flat_rows = jnp.concatenate(flat, axis=0)
        small = jnp.concatenate([flat_rows, flat_rows], axis=1)
        up_b_rows = jnp.concatenate([up_bias, jnp.zeros((14, hid_rows), bf16)], axis=0)
        wide = 3 * heads * size
        outs = [((2 * rows, wide), bf16), ((2 * rows + 16, wide), bf16)]
        outs = outs + [((2 * rows, hidden // 4), bf16)] * 2
        outs = outs + [((LAYERS, hid_rows // 2, width), bf16)]
        q_mine, q_theirs, u_mine, u_theirs, down_units = call(
            functools.partial(units_body, rows, heads, size),
            outs,
            [where, qkv_weight, up_weight, down_weight, small],
            0,
            smem=1,
        )
        q_side, u_side = core_swap(q_theirs), core_swap(u_theirs)
        p_side = x_swap(proj_weight, n)
        outs = [((2 * rows + 16, wide), bf16), ((2 * rows, wide), bf16)]
        outs = outs + [((2 * rows, hidden // 4), bf16)] * 2 + [((rows, width), bf16)] * 2
        q0, q1, u0, u1, p0, p1 = call(
            functools.partial(join_body, rows),
            outs,
            [where, q_mine, q_side, u_mine, u_side, small, up_b_rows, proj_weight, p_side],
            0,
            smem=1,
        )
        for layer, (q, u, p) in enumerate(((q0, u0, p0), (q1, u1, p1))):
            extra = 16 if layer == 0 else 0
            got = gather_rows(q, f, n, extra)
            if extra:
                shapes = [((16, width), f32), ((2 * LAYERS, wide), f32), ((16, hidden // 4), f32)]
                vec, fix, up_b = call(
                    functools.partial(prep_body, n, heads, size), shapes, [where, got[1]], 0, smem=1
                )
            weights.append(
                (
                    got[0],
                    gather_line(p, f, n),
                    gather_rows(u, f, n)[0],
                    gather_rows(down_units[layer], f, n)[0],
                )
            )
    else:
        packed = jnp.concatenate(flat + [up_bias], axis=1)
        everything = lax.all_gather(packed, ("fsdp", "seq"), axis=0)
        for layer in range(LAYERS):
            full = [
                lax.all_gather(w[layer], ("fsdp", "seq"), axis=0, tiled=True)
                for w in (qkv_weight, proj_weight, up_weight, down_weight)
            ]
            by_head = full[1].reshape(heads, 4, size, width)
            by_hid = full[3].reshape(n, 2, 2, hid_rows // 2, width)
            weights.append(
                (
                    qkv_cols(full[0], quarter),
                    pick(by_head, 1, quarter).reshape(heads * size, width),
                    up_cols(full[2], c, y),
                    pick(pick(by_hid, 2, y), 1, c).reshape(hidden // 4, width),
                )
            )

        vectors = everything[:, :, : 8 * rows].reshape(2 * n, LAYERS, 8, rows)
        vectors = widen(vectors.transpose(2, 1, 0, 3).reshape(8, LAYERS, width))
        vec = vectors.reshape(8 * LAYERS, width)
        up_b = everything[:, :, 8 * rows :].reshape(n, 2, LAYERS, 2, hid_rows // 2)
        up_b = pick(pick(up_b, 3, y), 1, c).transpose(1, 0, 2)
        up_b = widen(up_b.reshape(LAYERS, hidden // 4))
        by_head = vectors.reshape(8, LAYERS, heads, 4, size)
        by_head = pick(by_head, 3, quarter).reshape(8, LAYERS, heads * size)
        zero = jnp.zeros_like(by_head[0])
        add = jnp.concatenate([by_head[QUERY_B], zero, by_head[VALUE_B]], axis=1)
        times = jnp.concatenate([zero + 0.125, zero + 1.0, zero + 1.0], axis=1)
        fix = jnp.stack([add, times], axis=1).reshape(2 * LAYERS, -1)

    streams = range(2)
    sent = [None, None]
    stash = []
    for layer in range(LAYERS):
        w_qkv, w_proj, w_up, w_down = weights[layer]
        kept = []
        for s in streams:
            before, normed, qkv, attended, stat, low = attend(
                resid[s], sent[s], vec, w_qkv, fix, w_proj, layer, heads, size
            )
            got = send_part(low)
            mid, normed_two, active, slope = go_up(before, got, vec, w_up, up_b, layer)
            kept.append((before, normed, qkv, attended, mid, normed_two, slope, active, stat))
            sent[s] = send_part(go_down(active, w_down))
            resid[s] = mid
        stash.append(kept)

    def own_rows(pair):
        return jnp.where(y == 0, pair[0], pair[1])

    last_bias = vec[2 * DOWN_B + LAYERS - 1]
    clips_out = own_rows([r[:toks] for r in resid]) + (
        widen(own_rows([p[0][:toks] for p in sent]))
        + widen(own_rows([p[1][toks:] for p in sent]))
        + widen(own_rows([p[2] for p in sent]))
        + last_bias
    )
    clips_out = clips_out.astype(bf16)[None]

    grads = [None] * LAYERS
    tallies = [None] * LAYERS
    d_mid, sent = [None, None], [None, None]

    def both_t_mm(left, right):
        return t_mm(
            jnp.concatenate(left, axis=0), jnp.concatenate(right, axis=0)
        ).astype(bf16)

    for layer in reversed(range(LAYERS)):
        w_qkv, w_proj, w_up, w_down = weights[layer]
        kept = stash[layer]
        d_mlp, d_pre, d_branch, d_joined, grad = [], [], [], [], []
        ups, mlp, att, joined = [], [], [], []
        for s in streams:
            slope = kept[s][6]
            if layer == LAYERS - 1:
                got = (start[s], start[s]) + tuple(
                    mlp_back(start[s], None, None, None, None, slope, w_down, w_up, layer)
                )
            else:
                after = stash[layer + 1][s][0]
                got = mlp_back(None, after, d_mid[s], sent[s], vec, slope, w_down, w_up, layer)
            grad.append(got[0])
            d_mlp.append(got[1])
            d_pre.append(got[2])
            ups.append(got[4])
            mlp.append(got[5])
            sent[s] = send_part(got[3])
        g_down = both_t_mm([k[7] for k in kept], d_mlp)
        g_up = both_t_mm([k[5] for k in kept], d_pre)
        for s in streams:
            _, _, qkv, _, mid, _, _, _, stat = kept[s]
            got = attend_back(
                grad[s], mid, sent[s], vec, qkv, stat, w_proj, w_qkv, layer, heads, size
            )
            d_mid[s] = got[0]
            d_branch.append(got[1])
            d_joined.append(got[2])
            att.append(got[4])
            joined.append(got[5])
            sent[s] = send_part(got[3])
        g_proj = both_t_mm([k[3] for k in kept], d_branch)
        g_qkv = both_t_mm([k[1] for k in kept], d_joined)
        grads[layer] = (g_qkv, g_proj, g_up, g_down)
        tallies[layer] = [*ups, *mlp, *att, *joined]
    ends = [(stash[0][s][0], d_mid[s], *sent[s]) for s in streams]
    input_grad, first = last_back(where, ends, vec)
    input_grad = input_grad[None]

    if fast:
        tiny = call(
            functools.partial(pack_body, n, heads, size),
            [((n, 24, 2 * rows), f32)],
            [where, first, *tallies[1], *tallies[0]],
            0,
            smem=1,
        )[0]
        tiny = scatter(tiny.reshape(n * 24, 2 * rows), where, f, n)
        tiny = (tiny[0] + tiny[1]) + (tiny[2] + tiny[3])
        tiny = tiny + core_swap(tiny)
        tiny = tiny + y_swap(tiny)
        vecs = pick(tiny[:16].reshape(8, LAYERS, 2, rows), 2, c)
        ups = pick(tiny[16:].reshape(LAYERS, 2, 2 * 2 * rows), 1, c)
        outs = None
        for layer in reversed(range(LAYERS)):
            g_qkv, g_proj, g_up, g_down = grads[layer]
            d = both_types(scatter(g_down, where, f, n))
            d = (d[0], y_swap(d[1]))
            u = to_rows(scatter(g_up, where, f, n), where)
            q = to_rows(scatter(g_qkv, where, f, n), where)
            p = both_types(scatter(g_proj, where, f, n, True))
            side = x_swap(p[1], n)
            p = both_types([p[0], side])
            p = (p[0], y_swap(p[1]))
            outs = finish(where, q, u, d, p, outs, layer, n, heads, size)
        qkv_out, proj_out, up_out, down_out = outs
    else:
        here = (jnp.arange(4) == quarter).reshape(1, 1, 4, 1)
        at_c = (jnp.arange(2) == c).reshape(1, 2, 1, 1)
        at_y = (jnp.arange(2) == y).reshape(1, 1, 2, 1)

        def rows_of(pair, i):
            return jnp.sum(pair[0][8 * i : 8 * i + 8] + pair[1][8 * i : 8 * i + 8], axis=0)

        by_owner = []
        for layer in range(LAYERS):
            tally = tallies[layer]
            ups, mlp, att, joined = [tally[2 * i : 2 * i + 2] for i in range(4)]
            if layer == 0:
                one_sums = [jnp.sum(first[8 * i : 8 * i + 8], axis=0) for i in range(2)]
            else:
                one_sums = [rows_of(tallies[layer - 1][2:4], i) for i in range(2)]
            joined = rows_of(joined, 0).reshape(3, heads, 1, size)[0::2]
            joined = jnp.where(here, joined, 0.0).reshape(2, width)
            alike = [rows_of(mlp, 2), *one_sums, rows_of(att, 2), rows_of(att, 0), rows_of(att, 1)]
            alike = [0.25 * v for v in alike]
            vecs = [alike[1], alike[2], joined[0], joined[1], alike[3], alike[4], alike[5], alike[0]]
            vecs = jnp.stack(vecs).reshape(8, 2 * n, rows).transpose(1, 0, 2)
            up = rows_of(ups, 0).reshape(n, 1, 1, hid_rows // 2)
            up = jnp.where(at_c & at_y, up, 0.0).reshape(2 * n, hid_rows)
            by_owner.append(jnp.concatenate([vecs.reshape(2 * n, 8 * rows), up], axis=1))
        total = lax.psum(jnp.stack(by_owner, axis=1), ("fsdp", "seq", "replica"))
        tiny = pick(total, 0, 2 * f + c)
        vecs = tiny[:, : 8 * rows].reshape(LAYERS, 8, rows).transpose(1, 0, 2)
        ups = tiny[:, 8 * rows :]
        axes = ("replica", "seq")

        def owned(full):
            block = lax.psum_scatter(full, "fsdp", scatter_dimension=0, tiled=True)
            half = block.shape[0] // 2
            return widen(lax.dynamic_slice_in_dim(block, c * half, half, axis=0))

        outs = []
        for layer in range(LAYERS):
            g_qkv, g_proj, g_up, g_down = grads[layer]
            g = lax.all_gather(g_qkv, axes, axis=0).reshape(4, width, 3, heads, size)
            qkv_out = owned(g.transpose(1, 2, 3, 0, 4).reshape(width, 3 * width))
            g = lax.all_gather(g_proj, axes, axis=0).reshape(4, heads, size, width)
            proj_out = owned(g.transpose(1, 0, 2, 3).reshape(width, width))
            g = lax.all_gather(g_up, axes, axis=0)
            g = g.reshape(2, 2, width, n, hid_rows // 2)
            up_out = owned(g.transpose(2, 3, 1, 0, 4).reshape(width, hidden))
            g = lax.all_gather(g_down, axes, axis=0)
            g = g.reshape(2, 2, n, hid_rows // 2, width)
            down_out = owned(g.transpose(2, 1, 0, 3, 4).reshape(hidden, width))
            outs.append((qkv_out, proj_out, up_out, down_out))
        qkv_out, proj_out, up_out, down_out = [
            jnp.stack([outs[layer][i] for layer in range(LAYERS)]) for i in range(4)
        ]
    return (
        clips_out,
        input_grad,
        vecs[GAIN_ONE],
        vecs[SHIFT_ONE],
        qkv_out,
        vecs[QUERY_B],
        vecs[VALUE_B],
        proj_out,
        vecs[PROJ_B],
        vecs[GAIN_TWO],
        vecs[SHIFT_TWO],
        up_out,
        ups,
        down_out,
        vecs[DOWN_B],
    )


def solution(mesh):
    tokens = P(("fsdp", "replica"), "seq", None)
    vector = P(None, ("fsdp", "seq"))
    matrix = P(None, ("fsdp", "seq"), None)
    kinds = [
        vector,
        vector,
        matrix,
        vector,
        vector,
        matrix,
        vector,
        vector,
        vector,
        matrix,
        vector,
        matrix,
        vector,
    ]
    return jax.shard_map(
        functools.partial(on_device, n=mesh.shape["fsdp"]),
        mesh=mesh,
        in_specs=(tokens, tokens, P(("fsdp", "replica")), *kinds),
        out_specs=(tokens, tokens, *kinds),
        check_vma=False,
    )
```

```python
import functools

import jax
import jax.numpy as jnp
from jax import lax
from jax.experimental import pallas as pl
from jax.experimental.pallas import tpu as pltpu
from jax.sharding import PartitionSpec as P


HEADS = 16
LAYERS = 2
norm_eps = 1e-06
bf16 = jnp.bfloat16
f32 = jnp.float32


def widen(array):
    return array.astype(f32)


def dot(a, b, dims):
    return lax.dot_general(a, b, (dims, ((), ())), preferred_element_type=f32)


def mm(a, b):
    return dot(a, b, ((1,), (0,)))


def mm_t(a, b):
    return dot(a, b, ((1,), (1,)))


def t_mm(a, b):
    return dot(a, b, ((0,), (0,)))


PAIR = [(0, 1), (1, 0)]


def core_swap(v):
    return lax.ppermute(v, "seq", PAIR)


def y_swap(v):
    return lax.ppermute(v, "replica", PAIR)


def x_swap(v, n):
    return lax.ppermute(v, "fsdp", [(f, f ^ 1) for f in range(n)])


def z_from(v, k, n):
    nz = n // 2
    return lax.ppermute(
        v, "fsdp", [(((z + k) % nz) * 2 + x, z * 2 + x) for z in range(nz) for x in range(2)]
    )


def pick(array, axis, at):
    return lax.dynamic_index_in_dim(array, at, axis, keepdims=False)


TILE = 112
COLS = 256
VMEM_LIMIT = 20 * 1024 * 1024
HBM = pltpu.MemorySpace.HBM


def call(body, outs, args, flops, transcendentals=0, scratch=(), smem=0):
    shapes = tuple(jax.ShapeDtypeStruct(o[0], o[1]) for o in outs)
    far = [i for i, o in enumerate(outs) if len(o) > 2 and o[2]]
    n_in, n_out, n_far = len(args), len(outs), len(far)

    def run(*refs):
        out_refs = list(refs[n_in : n_in + n_out])
        rest = refs[n_in + n_out :]
        sems = rest[-1] if far else None
        copies = {}
        for j, i in enumerate(far):
            copies[i] = pltpu.make_async_copy(rest[j], out_refs[i], sems.at[j])
            out_refs[i] = rest[j]
        extra = rest[n_far:-1] if far else rest[n_far:]
        body(lambda i: copies[i].start(), *refs[:n_in], *out_refs, *extra)
        for copy in copies.values():
            copy.wait()

    touched = sum(a.size * a.dtype.itemsize for a in (*args, *shapes))
    scratch = [pltpu.VMEM(*outs[i][:2]) for i in far] + list(scratch)
    if far:
        scratch.append(pltpu.SemaphoreType.DMA((n_far,)))
    spaces = [pltpu.SMEM if i < smem else pltpu.VMEM for i in range(n_in)]
    return pl.pallas_call(
        run,
        out_shape=shapes,
        in_specs=[pl.BlockSpec(memory_space=s) for s in spaces],
        out_specs=tuple(
            pl.BlockSpec(memory_space=HBM if i in far else pltpu.VMEM) for i in range(n_out)
        ),
        scratch_shapes=scratch,
        compiler_params=pltpu.CompilerParams(vmem_limit_bytes=VMEM_LIMIT),
        cost_estimate=pl.CostEstimate(
            flops=flops, bytes_accessed=touched, transcendentals=transcendentals
        ),
    )(*args)


def norm_parts(inputs):
    center = inputs - jnp.mean(inputs, axis=-1, keepdims=True)
    spread = jnp.mean(center * center, axis=-1, keepdims=True)
    scale = lax.rsqrt(spread + norm_eps)
    return center * scale, scale


def norm_grad(e, inputs, gain):
    unit, scale = norm_parts(inputs)
    eg = e * gain
    d = scale * (
        eg
        - jnp.mean(eg, axis=-1, keepdims=True)
        - unit * jnp.mean(eg * unit, axis=-1, keepdims=True)
    )
    return d, e * unit


def eight(v):
    return jnp.sum(v.reshape(v.shape[0] // 8, 8, v.shape[1]), axis=0)


def one(v):
    return jnp.sum(v, axis=0, keepdims=True)


def by_rows(half_rows, step):
    for half in range(2):

        @pl.loop(0, half_rows // TILE)
        def _(i):
            start = pl.multiple_of(i * TILE, TILE)
            step(pl.ds(half * half_rows + start, TILE), half, pl.ds(start, TILE))


def by_cols(width, step):
    @pl.loop(0, width // COLS)
    def _(i):
        step(pl.ds(pl.multiple_of(i * COLS, COLS), COLS))


def summed(sent, whole, half, part):
    rows = sent[1].shape[0] // 2
    side = pl.ds((1 - half) * rows + part.start, TILE)
    total = widen(sent[0][whole, :]) + widen(sent[1][side, :])
    return total + widen(sent[2 + half][part, :])


def put(ref, cols, value):
    ref[:, cols] = value.astype(ref.dtype)


def heads_of(ref, width, size, h):
    return [ref[:, i * width + h * size : i * width + (h + 1) * size] for i in range(3)]


GAIN_ONE, SHIFT_ONE, QUERY_B, VALUE_B, PROJ_B, GAIN_TWO, SHIFT_TWO, DOWN_B = range(8)


def row(vec, which, layer):
    at = 2 * which + layer
    return vec[at : at + 1, :]


def attend_body(layer, heads, size, flush, *refs):
    if layer == 0:
        base, vec, w_qkv, fix, w_proj, normed, qkv, attended, stat, low = refs
        sent, shift = None, 0
    else:
        base, s0, s1, s2, s3, vec, w_qkv, fix, w_proj = refs[:9]
        resid, normed, qkv, attended, stat, low = refs[9:]
        sent, shift = (s0, s1, s2, s3), 1
    width = heads * size

    def norm(whole, half, part_rows):
        value = widen(base[whole, :])
        if sent is not None:
            value = value + (summed(sent, whole, half, part_rows) + row(vec, DOWN_B, layer - 1))
            resid[whole, :] = value
        unit, _ = norm_parts(value)
        normed[whole, :] = (
            unit * row(vec, GAIN_ONE, layer) + row(vec, SHIFT_ONE, layer)
        ).astype(bf16)

    by_rows(base.shape[0] // 2, norm)
    for i in range(shift + 1):
        flush(i)

    def project(cols):
        value = mm(normed[...], w_qkv[:, cols]) + fix[2 * layer : 2 * layer + 1, cols]
        qkv[:, cols] = (value * fix[2 * layer + 1 : 2 * layer + 2, cols]).astype(bf16)

    by_cols(3 * width, project)
    flush(shift + 1)
    for h in range(heads):
        q, k, v = heads_of(qkv, width, size, h)
        s = mm_t(q, k)
        peak = jnp.max(s, axis=-1, keepdims=True)
        e = jnp.exp(s - peak)
        total = jnp.sum(e, axis=-1, keepdims=True)
        value = mm(e.astype(bf16), v) * (1.0 / total)
        attended[:, h * size : (h + 1) * size] = value.astype(bf16)
        stat[:, h : h + 1] = peak + jnp.log(total)
    flush(shift + 2)
    flush(shift + 3)
    by_cols(low.shape[1], lambda cols: put(low, cols, mm(attended[...], w_proj[:, cols])))


def attend(base, sent, vec, w_qkv, fix, w_proj, layer, heads, size):
    toks, width = base.shape
    outs = [((toks, width), bf16, True), ((toks, 3 * heads * size), bf16, True)]
    outs = outs + [((toks, heads * size), bf16, True), ((toks, 128), f32, True)]
    outs = outs + [((toks, width), bf16)]
    if layer:
        outs = [((toks, width), f32, True)] + outs
    args = [base, *(sent or ()), vec, w_qkv, fix, w_proj]
    flops = 8 * toks * width * heads * size + 4 * heads * toks * toks * size
    body = functools.partial(attend_body, layer, heads, size)
    got = call(body, outs, args, flops, heads * toks * toks)
    return got if layer else (base, *got)


ROOT_HALF = 0.7071067811865476
ROOT_TWO_PI_INV = 0.3989422804014327


def up_body(layer, flush, base, s0, s1, s2, s3, vec, w_up, up_b, mid, normed, active, slope):
    def norm(whole, half, part_rows):
        value = widen(base[whole, :])
        value = value + (
            summed((s0, s1, s2, s3), whole, half, part_rows) + row(vec, PROJ_B, layer)
        )
        mid[whole, :] = value
        unit, _ = norm_parts(value)
        normed[whole, :] = (
            unit * row(vec, GAIN_TWO, layer) + row(vec, SHIFT_TWO, layer)
        ).astype(bf16)

    by_rows(base.shape[0] // 2, norm)
    flush(0)
    flush(1)

    def up(cols):
        pre = mm(normed[...], w_up[:, cols]) + up_b[layer : layer + 1, cols]
        half = 0.5 * (1.0 + lax.erf(pre * ROOT_HALF))
        put(active, cols, pre * half)
        put(slope, cols, half + pre * (ROOT_TWO_PI_INV * jnp.exp(-0.5 * pre * pre)))

    by_cols(w_up.shape[1], up)
    flush(2)
    flush(3)


def go_up(base, sent, vec, w_up, up_b, layer):
    toks, width = base.shape
    hid = w_up.shape[1]
    outs = [((toks, width), f32, True), ((toks, width), bf16, True)]
    outs = outs + [((toks, hid), bf16, True), ((toks, hid), bf16, True)]
    args = [base, *sent, vec, w_up, up_b]
    body = functools.partial(up_body, layer)
    return call(body, outs, args, 2 * toks * width * hid, toks * hid)


def down_body(flush, active, w_down, low):
    by_cols(low.shape[1], lambda cols: put(low, cols, mm(active[...], w_down[:, cols])))


def go_down(active, w_down):
    outs = [((active.shape[0], w_down.shape[1]), bf16)]
    flops = 2 * active.size * w_down.shape[1]
    return call(down_body, outs, [active, w_down], flops)[0]


def mlp_back_tail(flush, at, d_mlp, slope, w_down, w_up, d_pre, low, up_sum):
    def back(cols):
        value = (mm_t(d_mlp[...], w_down[cols, :]) * widen(slope[:, cols])).astype(bf16)
        d_pre[:, cols] = value
        up_sum[:, cols] = eight(widen(value))

    by_cols(w_down.shape[0], back)
    flush(at)
    by_cols(low.shape[1], lambda cols: put(low, cols, mm_t(d_pre[...], w_up[cols, :])))


def mlp_back_first(flush, d_mlp, slope, w_down, w_up, d_pre, low, up_sum, sums):
    sums[...] = jnp.zeros_like(sums)

    def count(whole, half, part_rows):
        sums[16:24, :] += eight(widen(d_mlp[whole, :]))

    by_rows(d_mlp.shape[0] // 2, count)
    mlp_back_tail(flush, 0, d_mlp, slope, w_down, w_up, d_pre, low, up_sum)


def mlp_back_body(layer, flush, base, d_mid, s0, s1, s2, s3, vec, slope, w_down, w_up, *outs):
    grad, d_mlp, d_pre, low, up_sum, sums = outs
    sums[...] = jnp.zeros_like(sums)

    def norm(whole, half, part_rows):
        e = summed((s0, s1, s2, s3), whole, half, part_rows)
        d, by_gain = norm_grad(e, widen(base[whole, :]), row(vec, GAIN_ONE, layer + 1))
        value = d_mid[whole, :] + d
        grad[whole, :] = value
        low_value = value.astype(bf16)
        d_mlp[whole, :] = low_value
        sums[0:8, :] += eight(by_gain)
        sums[8:16, :] += eight(e)
        sums[16:24, :] += eight(widen(low_value))

    by_rows(base.shape[0] // 2, norm)
    flush(0)
    flush(1)
    mlp_back_tail(flush, 2, d_mlp, slope, w_down, w_up, d_pre, low, up_sum)


def mlp_back(first, base, d_mid, sent, vec, slope, w_down, w_up, layer):
    toks, hid = slope.shape
    width = w_up.shape[0]
    outs = [((toks, hid), bf16, True), ((toks, width), bf16), ((8, hid), f32), ((24, width), f32)]
    flops = 4 * toks * hid * width
    if first is not None:
        return call(mlp_back_first, outs, [first, slope, w_down, w_up], flops)
    outs = [((toks, width), f32, True), ((toks, width), bf16, True), *outs]
    args = [base, d_mid, *sent, vec, slope, w_down, w_up]
    return call(functools.partial(mlp_back_body, layer), outs, args, flops)


def attend_back_body(layer, heads, size, flush, *refs):
    grad, mid, s0, s1, s2, s3, vec, qkv, stat, w_proj, w_qkv = refs[:11]
    d_mid, d_branch, d_joined, low, sums, joined_sum, d_att = refs[11:]
    width = heads * size
    sums[...] = jnp.zeros_like(sums)

    def norm(whole, half, part_rows):
        e = summed((s0, s1, s2, s3), whole, half, part_rows)
        d, by_gain = norm_grad(e, mid[whole, :], row(vec, GAIN_TWO, layer))
        value = widen(grad[whole, :]) + d
        d_mid[whole, :] = value
        low_value = value.astype(bf16)
        d_branch[whole, :] = low_value
        sums[0:8, :] += eight(by_gain)
        sums[8:16, :] += eight(e)
        sums[16:24, :] += eight(widen(low_value))

    by_rows(mid.shape[0] // 2, norm)
    flush(0)
    flush(1)
    d_att[...] = mm_t(d_branch[...], w_proj[...]).astype(bf16)
    rows = stat[...].T
    for h in range(heads):
        q, k, v = heads_of(qkv, width, size, h)
        d = d_att[:, h * size : (h + 1) * size]
        p = jnp.exp(mm_t(k, q) - rows[h : h + 1, :])
        dv = mm(p.astype(bf16), d)
        d_p = mm_t(v, d)
        ds = (p * (d_p - jnp.sum(p * d_p, axis=0, keepdims=True))).astype(bf16)
        dk = mm(ds, q)
        dq = widen(t_mm(ds, k).astype(bf16)) * 0.125
        for i, value in enumerate((dq, dk, dv)):
            at = i * width + h * size
            d_joined[:, at : at + size] = value.astype(bf16)
    flush(2)
    joined_sum[...] = eight(widen(d_joined[...]))
    by_cols(low.shape[1], lambda cols: put(low, cols, mm_t(d_joined[...], w_qkv[cols, :])))


def attend_back(grad, mid, sent, vec, qkv, stat, w_proj, w_qkv, layer, heads, size):
    toks, width = mid.shape
    wide = 3 * heads * size
    outs = [((toks, width), f32, True), ((toks, width), bf16, True), ((toks, wide), bf16, True)]
    outs = outs + [((toks, width), bf16), ((24, width), f32), ((8, wide), f32)]
    args = [grad, mid, *sent, vec, qkv, stat, w_proj, w_qkv]
    flops = 8 * toks * width * heads * size + 10 * heads * toks * toks * size
    return call(
        functools.partial(attend_back_body, layer, heads, size),
        outs,
        args,
        flops,
        heads * toks * toks,
        [pltpu.VMEM((toks, heads * size), bf16)],
    )


def last_body(flush, where, *refs):
    streams, vec, grad, sums = (refs[0:6], refs[6:12]), refs[12], refs[13], refs[14]
    sums[...] = jnp.zeros_like(sums)
    for s, (base, d_mid, *sent) in enumerate(streams):

        def norm(whole, half, part_rows):
            e = summed(sent, whole, half, part_rows)
            d, by_gain = norm_grad(e, widen(base[whole, :]), row(vec, GAIN_ONE, 0))
            sums[0:8, :] += eight(by_gain)
            sums[8:16, :] += eight(e)
            if half == 0:

                @pl.when(where[1] == s)
                def _():
                    grad[part_rows, :] = d_mid[whole, :] + d

        by_rows(base.shape[0] // 2, norm)
    flush(0)


def last_back(where, streams, vec):
    toks, width = streams[0][0].shape
    outs = [((toks // 2, width), f32, True), ((16, width), f32)]
    args = [where, *streams[0], *streams[1], vec]
    return call(last_body, outs, args, 20 * toks * width, smem=1)


def pick_body(toks, flush, where, own, side, across, beside, *outs):
    for i in range(2):
        at = slice(i * toks, (i + 1) * toks)
        for s in range(2):
            out = outs[2 * i + s]

            @pl.when(where[1] == s)
            def _():
                out[0:toks, :] = own[at, :]
                out[toks:, :] = side[at, :]

            @pl.when(where[1] != s)
            def _():
                out[0:toks, :] = across[at, :]
                out[toks:, :] = beside[at, :]

            flush(2 * i + s)


def halves(first, second, c):
    low = lax.broadcasted_iota(jnp.int32, first.shape, 1) < first.shape[1] // 2
    half = first.shape[1] // 2
    zero = jnp.where(low, first, pltpu.roll(second, half, 1))
    other = jnp.where(low, pltpu.roll(first, half, 1), second)
    return jnp.where(c == 0, zero, other), jnp.where(c == 0, other, zero)


def units_body(rows, heads, size, flush, where, qkv, up, down, small, *outs):
    q_mine, q_theirs, u_mine, u_theirs, d_unit = outs
    c, y = where[0], where[1]
    pair = 2 * size
    for layer in range(LAYERS):
        at = slice(layer * rows, (layer + 1) * rows)
        for t in range(3):
            for h in range(0, heads, 2):
                start = (t * heads + h) * 2 * pair
                tiles = [
                    widen(qkv[layer, :, pl.ds(pl.multiple_of(start + i * 2 * pair + y * pair, pair), pair)])
                    for i in range(2)
                ]
                mine, theirs = halves(*tiles, c)
                cols = slice((t * heads + h) * size, (t * heads + h + 2) * size)
                q_mine[at, cols] = mine.astype(bf16)
                q_theirs[at, cols] = theirs.astype(bf16)
        blocks = up.shape[2] // (4 * pair)
        for f in range(blocks):
            for ref, core in ((u_mine, c), (u_theirs, 1 - c)):
                start = pl.multiple_of(f * 4 * pair + core * 2 * pair + y * pair, pair)
                ref[at, f * pair : (f + 1) * pair] = up[layer, :, pl.ds(start, pair)]
        half = down.shape[1] // 2
        d_unit[layer] = down[layer, pl.ds(pl.multiple_of(y * half, half), half), :]
    q_theirs[2 * rows :, :] = jnp.zeros((16, q_theirs.shape[1]), bf16)
    q_theirs[2 * rows :, 0:pair] = small[...]


def join_body(rows, flush, where, q_mine, q_side, u_mine, u_side, small, up_b, q0, q1, u0, u1):
    c, y = where[0], where[1]
    pair = small.shape[1]
    here = pl.ds(pl.multiple_of(c * rows, rows), rows)
    there = pl.ds(pl.multiple_of((1 - c) * rows, rows), rows)
    for layer, (q, u) in enumerate(((q0, u0), (q1, u1))):
        at = slice(layer * rows, (layer + 1) * rows)
        q[here, :] = q_mine[at, :]
        q[there, :] = q_side[at, :]
        u[here, :] = u_mine[at, :]
        u[there, :] = u_side[at, :]
    low = lax.broadcasted_iota(jnp.int32, small.shape, 1) < pair // 2
    own, side = widen(small[...]), widen(q_side[2 * rows :, 0:pair])
    both = jnp.where(c == 0, jnp.where(low, own, side), jnp.where(low, side, own))
    q0[2 * rows :, :] = jnp.zeros((16, q0.shape[1]), bf16)
    q0[2 * rows :, 0:pair] = both.astype(bf16)
    ups = widen(up_b[...])
    ups = jnp.where(y == 0, ups[:, 0:pair], ups[:, pair : 2 * pair])
    q0[2 * rows :, pair : 2 * pair] = ups.astype(bf16)


def choose_body(flush, where, own, side, *outs):
    x, y = where[2], where[1]
    for layer, out in enumerate(outs):

        @pl.when(x == y)
        def _():
            out[...] = own[layer]

        @pl.when(x != y)
        def _():
            out[...] = side[layer]


def prep_body(n, heads, size, flush, where, small, vec, fix, up_b):
    c, y = where[0], where[1]
    pair = 2 * size
    for f in range(n):
        vec[:, f * pair : (f + 1) * pair] = widen(small[:, f * 2 * pair : f * 2 * pair + pair])
        up_b[:, f * pair : (f + 1) * pair] = widen(
            small[:, f * 2 * pair + pair : (f + 1) * 2 * pair]
        )
    width = heads * size
    for layer in range(LAYERS):
        for t, which in ((0, QUERY_B), (2, VALUE_B)):
            for i in range(0, heads, 2):
                tiles = [
                    widen(small[:, pl.ds(pl.multiple_of((2 * (i + j) + y) * 2 * pair, 2 * pair), pair)])
                    for j in range(2)
                ]
                mine, _ = halves(*tiles, c)
                at = 2 * which + layer
                start = t * width + i * size
                fix[2 * layer : 2 * layer + 1, start : start + pair] = mine[at : at + 1, :]
        fix[2 * layer : 2 * layer + 1, width : 2 * width] = jnp.zeros((1, width), f32)
        fix[2 * layer + 1 : 2 * layer + 2, 0:width] = jnp.full((1, width), 0.125, f32)
        fix[2 * layer + 1 : 2 * layer + 2, width:] = jnp.ones((1, 2 * width), f32)


def place_body(count, rows, extra, at_ref, *refs):
    n_out = 2 if extra else 1
    blocks, outs, sems = refs[: -1 - n_out], refs[-1 - n_out : -1], refs[-1]
    copies = []
    per = count // len(blocks)
    for i in range(count):
        source, base = blocks[i // per], (i % per) * (rows + extra)
        start = pl.multiple_of(at_ref[i] * rows, rows)
        copies.append(
            pltpu.make_async_copy(
                source.at[pl.ds(base, rows)], outs[0].at[pl.ds(start, rows)], sems.at[0, i]
            )
        )
        if extra:
            start = pl.multiple_of(at_ref[i] * 256, 256)
            copies.append(
                pltpu.make_async_copy(
                    source.at[pl.ds(base + rows, extra), pl.ds(0, 256)],
                    outs[1].at[:, pl.ds(start, 256)],
                    sems.at[1, i],
                )
            )
    for copy in copies:
        copy.start()
    for copy in copies:
        copy.wait()


def place(blocks, at, count, extra):
    total, cols = sum(b.shape[0] for b in blocks), blocks[0].shape[1]
    rows = total // count - extra
    outs = [jax.ShapeDtypeStruct((count * rows, cols), bf16)]
    if extra:
        outs.append(jax.ShapeDtypeStruct((extra, count * 256), bf16))
    return pl.pallas_call(
        functools.partial(place_body, count, rows, extra),
        in_specs=[pl.BlockSpec(memory_space=pltpu.SMEM)]
        + [pl.BlockSpec(memory_space=pltpu.VMEM)] * len(blocks),
        out_specs=tuple([pl.BlockSpec(memory_space=pl.ANY)] * len(outs)),
        scratch_shapes=[pltpu.SemaphoreType.DMA((2, count))],
        out_shape=tuple(outs),
        compiler_params=pltpu.CompilerParams(vmem_limit_bytes=VMEM_LIMIT),
        cost_estimate=pl.CostEstimate(flops=0, bytes_accessed=4 * total * cols, transcendentals=0),
        name="place",
    )(at, *blocks)


def z_pair(v, bit, n):
    return lax.ppermute(v, "fsdp", [(f, f ^ (2 * bit)) for f in range(n)])


def gather_first(unit, me, n, extra):
    nz = n // 2
    line = [unit] + [z_from(unit, k, n) for k in range(1, nz)]
    line = jnp.concatenate(line, axis=0)
    other = x_swap(line, n)
    z, x = me // 2, me % 2
    at = [((z + k) % nz) * 2 + x for k in range(nz)]
    at = at + [((z + k) % nz) * 2 + 1 - x for k in range(nz)]
    return place([line, other], jnp.stack(at).astype(jnp.int32), n, extra)


def along_z(unit, n):
    pair = z_pair(unit, 1, n)
    near = jnp.concatenate([unit, pair], axis=0)
    return near, z_pair(near, 2, n)


def gather_rows(unit, me, n):
    near, far = along_z(unit, n)
    near_x = x_swap(near, n)
    far_x = x_swap(far, n)
    z, x = me // 2, me % 2
    at = [(z ^ k) * 2 + x for k in range(4)] + [(z ^ k) * 2 + 1 - x for k in range(4)]
    at = jnp.stack(at).astype(jnp.int32)
    return place([near, far, near_x, far_x], at, n, 0)


def gather_line(unit, me, n):
    near, far = along_z(unit, n)
    at = jnp.stack([(me // 2) ^ k for k in range(4)]).astype(jnp.int32)
    return place([near, far], at, 4, 0)[0]


def split_body(nz, flush, where, *refs):
    grad, other = (refs[0], refs[1]) if len(refs) == 2 + nz else (refs[0], None)
    outs = refs[-nz:]
    x, z = where[2], where[3]
    rows = outs[0].shape[0]
    for k in range(nz):
        to = lax.rem(z - k + nz, nz)
        if other is None:
            value = grad[pl.ds(pl.multiple_of(to * rows, rows), rows), :]
        else:
            mine = grad[pl.ds(pl.multiple_of((to * 2 + x) * rows, rows), rows), :]
            value = widen(mine) + widen(other[pl.ds(pl.multiple_of(to * rows, rows), rows), :])
        outs[k][...] = value.astype(outs[k].dtype)


def scatter(grad, where, me, n, line=False):
    nz = n // 2
    count = nz if line else n
    rows, cols = grad.shape[0] // count, grad.shape[1]
    args = [where, grad]
    if not line:
        blocks = grad.reshape(nz, 2, rows, cols)
        sent = pick(blocks, 1, 1 - me % 2).reshape(nz * rows, cols)
        args.append(x_swap(sent, n))
    outs = [((rows, cols), f32)] + [((rows, cols), grad.dtype)] * (nz - 1)
    got = call(functools.partial(split_body, nz), outs, args, grad.size, smem=1)
    return [got[0]] + [z_from(got[k], k, n) for k in range(1, nz)]


def total_of(refs):
    total = widen(refs[0][...])
    for ref in refs[1:]:
        total = total + widen(ref[...])
    return total


def rows_body(rows, flush, where, *refs):
    mine, sent, total = refs[-3:]
    value = refs[0][...]
    for ref in refs[1:-3]:
        value = value + widen(ref[ref.shape[0] - 2 * rows :, :])
    total[...] = value
    c = where[0]
    mine[...] = total[pl.ds(pl.multiple_of(c * rows, rows), rows), :]
    sent[0:rows, :] = mine[...].astype(bf16)
    other = total[pl.ds(pl.multiple_of((1 - c) * rows, rows), rows), :]
    sent[rows:, :] = other.astype(bf16)


def to_rows(pieces, where):
    rows, cols = pieces[0].shape[0] // 2, pieces[0].shape[1]
    outs = [((rows, cols), f32), ((2 * rows, cols), bf16)]
    mine, sent = call(
        functools.partial(rows_body, rows),
        outs,
        [where, *pieces],
        4 * sent_size(pieces),
        scratch=[pltpu.VMEM((2 * rows, cols), f32)],
        smem=1,
    )
    across = y_swap(sent)
    side = core_swap(sent[rows:])
    beyond = core_swap(across[rows:])
    return mine, side, across, beyond


def sent_size(pieces):
    return sum(p.size for p in pieces)


def sum_body(flush, *refs):
    total = total_of(refs[:-2])
    refs[-2][...] = total
    refs[-1][...] = total.astype(refs[-1].dtype)


def both_types(pieces):
    shape = pieces[0].shape
    return call(sum_body, [(shape, f32), (shape, bf16)], list(pieces), sent_size(pieces))


def finish_body(layer, n, heads, size, first, where, *refs):
    q, u = refs[0:4], refs[4:8]
    d_own, d_side, p_own, p_side = refs[8:12]
    outs = refs[12 if first else 16 :][:4]
    b_q, b_p, b_u, b_d, sems = refs[-5:]
    c, y, x = where[0], where[1], where[2]
    pair = 2 * size
    rows = q[0].shape[0]

    def quarters(pieces, cols):
        mine, side = pieces[0][:, cols], widen(pieces[1][:, cols])
        across, beyond = widen(pieces[2][0:rows, cols]), widen(pieces[3][:, cols])
        here = (jnp.where(c == 0, mine, side), jnp.where(c == 0, side, mine))
        there = (jnp.where(c == 0, across, beyond), jnp.where(c == 0, beyond, across))
        return [
            [jnp.where(y == at, here[core], there[core]) for core in range(2)] for at in range(2)
        ]

    def out(i, buffer):
        return pltpu.make_async_copy(buffer, outs[i].at[layer], sems.at[i])

    for t in range(3):
        for h in range(0, heads, 2):
            at = (t * heads + h) * size
            got = quarters(q, slice(at, at + pair))
            for across in range(2):
                one_head, next_head = halves(*got[across], 0)
                start = (t * heads + h) * 2 * pair + across * pair
                b_q[:, start : start + pair] = one_head
                b_q[:, start + 2 * pair : start + 3 * pair] = next_head
    out(0, b_q).start()
    for f in range(n):
        got = quarters(u, slice(f * pair, (f + 1) * pair))
        for across in range(2):
            for core in range(2):
                start = f * 4 * pair + core * 2 * pair + across * pair
                b_u[:, start : start + pair] = got[across][core]
    out(2, b_u).start()
    half = d_own.shape[0]
    b_d[pl.ds(pl.multiple_of(y * half, half), half), :] = d_own[...]
    b_d[pl.ds(pl.multiple_of((1 - y) * half, half), half), :] = widen(d_side[...])
    out(3, b_d).start()
    b_p[...] = jnp.where(x == y, p_own[...], widen(p_side[...]))
    out(1, b_p).start()
    for i, buffer in enumerate((b_q, b_p, b_u, b_d)):
        out(i, buffer).wait()


def finish(where, q, u, d, p, past, layer, n, heads, size):
    rows = q[0].shape[0]
    width = HEADS * size
    hid = n * 8 * size
    shapes = [(rows, 3 * width), (rows, width), (rows, hid), (2 * d[0].shape[0], width)]
    args = [where, *q, *u, *d, *p]
    aliases = {}
    if past is not None:
        aliases = {len(args) + i: i for i in range(4)}
        args = args + list(past)
    first = past is None
    spaces = [pltpu.SMEM] + [pltpu.VMEM] * 12 + [HBM] * (0 if first else 4)
    return pl.pallas_call(
        functools.partial(finish_body, layer, n, heads, size, first),
        out_shape=tuple(jax.ShapeDtypeStruct((LAYERS, *s), f32) for s in shapes),
        in_specs=[pl.BlockSpec(memory_space=s) for s in spaces],
        out_specs=tuple([pl.BlockSpec(memory_space=HBM)] * 4),
        scratch_shapes=[pltpu.VMEM(s, f32) for s in shapes]
        + [pltpu.SemaphoreType.DMA((4,))],
        input_output_aliases=aliases,
        compiler_params=pltpu.CompilerParams(vmem_limit_bytes=VMEM_LIMIT),
        cost_estimate=pl.CostEstimate(
            flops=0, bytes_accessed=4 << 20, transcendentals=0
        ),
        name="finish",
    )(*args)


def pack_body(n, heads, size, flush, where, *refs):
    first, upper, lower, out = refs[0], refs[1:9], refs[9:17], refs[17]
    c, y = where[0], where[1]
    pair = 2 * size
    out[...] = jnp.zeros_like(out)

    def rows_of(ref, i):
        return one(ref[8 * i : 8 * i + 8, :])

    def put_vector(which, layer, value):
        at = 2 * which + layer
        for f in range(n):
            out[f, at : at + 1, :] = 0.25 * value[:, f * pair : (f + 1) * pair]

    def both(refs_of, i):
        return rows_of(refs_of[0], i) + rows_of(refs_of[1], i)

    for layer, group in ((1, upper), (0, lower)):
        ups, mlp, att, joined = group[0:2], group[2:4], group[4:6], group[6:8]
        put_vector(DOWN_B, layer, both(mlp, 2))
        put_vector(GAIN_TWO, layer, both(att, 0))
        put_vector(SHIFT_TWO, layer, both(att, 1))
        put_vector(PROJ_B, layer, both(att, 2))
        value = one(ups[0][...]) + one(ups[1][...])
        at = 16 + 4 * layer + 2 * c + y
        for f in range(n):
            out[f, pl.ds(at, 1), :] = value[:, f * pair : (f + 1) * pair]
        value = one(joined[0][...]) + one(joined[1][...])
        low = lax.broadcasted_iota(jnp.int32, (1, pair), 1) < size
        for t, which in ((0, QUERY_B), (2, VALUE_B)):
            at = 2 * which + layer
            for i in range(0, heads, 2):
                start = (t * heads + i) * size
                tile = value[:, start : start + pair]
                turned = pltpu.roll(jnp.broadcast_to(tile, (8, pair)), size, 1)[0:1, :]
                zero = jnp.zeros_like(tile)
                even = jnp.where(c == 0, jnp.where(low, tile, zero), jnp.where(low, zero, turned))
                odd = jnp.where(c == 0, jnp.where(low, turned, zero), jnp.where(low, zero, tile))
                out[2 * i + y, at : at + 1, :] = even
                out[2 * (i + 1) + y, at : at + 1, :] = odd
    mlp = lower[2:4]
    put_vector(GAIN_ONE, 1, both(mlp, 0))
    put_vector(SHIFT_ONE, 1, both(mlp, 1))
    put_vector(GAIN_ONE, 0, rows_of(first, 0))
    put_vector(SHIFT_ONE, 0, rows_of(first, 1))


def send_part(low):
    side = core_swap(low)
    half = low.shape[0] // 2
    mine = (widen(low[:half]) + widen(side[half:])).astype(bf16)
    across = y_swap(mine)
    beside = core_swap(across)
    return low, side, across, beside


def on_device(
    clips_in,
    cotangent,
    clip_mask,
    norm1_gain,
    norm1_bias,
    qkv_weight,
    query_bias,
    value_bias,
    proj_weight,
    proj_bias,
    norm2_gain,
    norm2_bias,
    up_weight,
    up_bias,
    down_weight,
    down_bias,
    *,
    n,
):
    c, y, f = lax.axis_index("seq"), lax.axis_index("replica"), lax.axis_index("fsdp")
    quarter = 2 * y + c
    toks, width = clips_in.shape[1], clips_in.shape[2]
    rows = qkv_weight.shape[1]
    hid_rows = down_weight.shape[1]
    hidden = up_weight.shape[2]
    size = width // HEADS
    heads = HEADS // 4
    fast = n == 8 and rows == size and hid_rows == 4 * rows

    where = jnp.stack([c, y, f % 2, f // 2]).astype(jnp.int32)

    masked = (widen(cotangent[0]) * widen(clip_mask)[0]).astype(bf16)
    own = jnp.concatenate([clips_in[0], masked], axis=0)
    side = core_swap(own)
    across = y_swap(own)
    beside = core_swap(across)
    got = call(
        functools.partial(pick_body, toks),
        [((2 * toks, width), bf16, True)] * 4,
        [where, own, side, across, beside],
        0,
        smem=1,
    )
    resid, start = list(got[:2]), got[2:]

    def qkv_cols(w, at):
        w = w.reshape(*w.shape[:-1], 3, heads, 4, size)
        return pick(w, w.ndim - 2, at).reshape(*w.shape[:-4], 3 * heads * size)

    def up_cols(w, at_c, at_y):
        w = w.reshape(*w.shape[:-1], n, 2, 2, hid_rows // 2)
        w = pick(w, w.ndim - 2, at_y)
        return pick(w, w.ndim - 2, at_c).reshape(*w.shape[:-3], hidden // 4)

    flat = [
        norm1_gain,
        norm1_bias,
        query_bias,
        value_bias,
        proj_bias,
        norm2_gain,
        norm2_bias,
        down_bias,
    ]
    weights = []
    if fast:
        flat_rows = jnp.concatenate(flat, axis=0)
        small = jnp.concatenate([flat_rows, flat_rows], axis=1)
        up_b_rows = jnp.concatenate([up_bias, jnp.zeros((14, hid_rows), bf16)], axis=0)
        wide = 3 * heads * size
        outs = [((2 * rows, wide), bf16), ((2 * rows + 16, wide), bf16)]
        outs = outs + [((2 * rows, hidden // 4), bf16)] * 2
        outs = outs + [((LAYERS, hid_rows // 2, width), bf16)]
        q_mine, q_theirs, u_mine, u_theirs, down_units = call(
            functools.partial(units_body, rows, heads, size),
            outs,
            [where, qkv_weight, up_weight, down_weight, small],
            0,
            smem=1,
        )
        q_side, u_side = core_swap(q_theirs), core_swap(u_theirs)
        outs = [((2 * rows + 16, wide), bf16), ((2 * rows, wide), bf16)]
        outs = outs + [((2 * rows, hidden // 4), bf16)] * 2
        q0, q1, u0, u1 = call(
            functools.partial(join_body, rows),
            outs,
            [where, q_mine, q_side, u_mine, u_side, small, up_b_rows],
            0,
            smem=1,
        )
        p_side = x_swap(proj_weight, n)
        p0, p1 = call(
            choose_body, [((rows, width), bf16)] * 2, [where, proj_weight, p_side], 0, smem=1
        )
        for layer, (q, u, p) in enumerate(((q0, u0, p0), (q1, u1, p1))):
            if layer:
                got = gather_rows(q, f, n)
            else:
                got = gather_first(q, f, n, 16)
                shapes = [((16, width), f32), ((2 * LAYERS, wide), f32), ((16, hidden // 4), f32)]
                vec, fix, up_b = call(
                    functools.partial(prep_body, n, heads, size), shapes, [where, got[1]], 0, smem=1
                )
            weights.append(
                (
                    got[0],
                    gather_line(p, f, n),
                    gather_rows(u, f, n)[0],
                    gather_rows(down_units[layer], f, n)[0],
                )
            )
    else:
        packed = jnp.concatenate(flat + [up_bias], axis=1)
        everything = lax.all_gather(packed, ("fsdp", "seq"), axis=0)
        for layer in range(LAYERS):
            full = [
                lax.all_gather(w[layer], ("fsdp", "seq"), axis=0, tiled=True)
                for w in (qkv_weight, proj_weight, up_weight, down_weight)
            ]
            by_head = full[1].reshape(heads, 4, size, width)
            by_hid = full[3].reshape(n, 2, 2, hid_rows // 2, width)
            weights.append(
                (
                    qkv_cols(full[0], quarter),
                    pick(by_head, 1, quarter).reshape(heads * size, width),
                    up_cols(full[2], c, y),
                    pick(pick(by_hid, 2, y), 1, c).reshape(hidden // 4, width),
                )
            )

        vectors = everything[:, :, : 8 * rows].reshape(2 * n, LAYERS, 8, rows)
        vectors = widen(vectors.transpose(2, 1, 0, 3).reshape(8, LAYERS, width))
        vec = vectors.reshape(8 * LAYERS, width)
        up_b = everything[:, :, 8 * rows :].reshape(n, 2, LAYERS, 2, hid_rows // 2)
        up_b = pick(pick(up_b, 3, y), 1, c).transpose(1, 0, 2)
        up_b = widen(up_b.reshape(LAYERS, hidden // 4))
        by_head = vectors.reshape(8, LAYERS, heads, 4, size)
        by_head = pick(by_head, 3, quarter).reshape(8, LAYERS, heads * size)
        zero = jnp.zeros_like(by_head[0])
        add = jnp.concatenate([by_head[QUERY_B], zero, by_head[VALUE_B]], axis=1)
        times = jnp.concatenate([zero + 0.125, zero + 1.0, zero + 1.0], axis=1)
        fix = jnp.stack([add, times], axis=1).reshape(2 * LAYERS, -1)

    streams = range(2)
    sent = [None, None]
    stash = []
    for layer in range(LAYERS):
        w_qkv, w_proj, w_up, w_down = weights[layer]
        kept = []
        for s in streams:
            before, normed, qkv, attended, stat, low = attend(
                resid[s], sent[s], vec, w_qkv, fix, w_proj, layer, heads, size
            )
            got = send_part(low)
            mid, normed_two, active, slope = go_up(before, got, vec, w_up, up_b, layer)
            kept.append((before, normed, qkv, attended, mid, normed_two, slope, active, stat))
            sent[s] = send_part(go_down(active, w_down))
            resid[s] = mid
        stash.append(kept)

    def own_rows(pair):
        return jnp.where(y == 0, pair[0], pair[1])

    last_bias = vec[2 * DOWN_B + LAYERS - 1]
    clips_out = own_rows([r[:toks] for r in resid]) + (
        widen(own_rows([p[0][:toks] for p in sent]))
        + widen(own_rows([p[1][toks:] for p in sent]))
        + widen(own_rows([p[2] for p in sent]))
        + last_bias
    )
    clips_out = clips_out.astype(bf16)[None]

    grads = [None] * LAYERS
    tallies = [None] * LAYERS
    d_mid, sent = [None, None], [None, None]

    def both_t_mm(left, right):
        return t_mm(
            jnp.concatenate(left, axis=0), jnp.concatenate(right, axis=0)
        ).astype(bf16)

    for layer in reversed(range(LAYERS)):
        w_qkv, w_proj, w_up, w_down = weights[layer]
        kept = stash[layer]
        d_mlp, d_pre, d_branch, d_joined, grad = [], [], [], [], []
        ups, mlp, att, joined = [], [], [], []
        for s in streams:
            slope = kept[s][6]
            if layer == LAYERS - 1:
                got = (start[s], start[s]) + tuple(
                    mlp_back(start[s], None, None, None, None, slope, w_down, w_up, layer)
                )
            else:
                after = stash[layer + 1][s][0]
                got = mlp_back(None, after, d_mid[s], sent[s], vec, slope, w_down, w_up, layer)
            grad.append(got[0])
            d_mlp.append(got[1])
            d_pre.append(got[2])
            ups.append(got[4])
            mlp.append(got[5])
            sent[s] = send_part(got[3])
        g_down = both_t_mm([k[7] for k in kept], d_mlp)
        g_up = both_t_mm([k[5] for k in kept], d_pre)
        for s in streams:
            _, _, qkv, _, mid, _, _, _, stat = kept[s]
            got = attend_back(
                grad[s], mid, sent[s], vec, qkv, stat, w_proj, w_qkv, layer, heads, size
            )
            d_mid[s] = got[0]
            d_branch.append(got[1])
            d_joined.append(got[2])
            att.append(got[4])
            joined.append(got[5])
            sent[s] = send_part(got[3])
        g_proj = both_t_mm([k[3] for k in kept], d_branch)
        g_qkv = both_t_mm([k[1] for k in kept], d_joined)
        grads[layer] = (g_qkv, g_proj, g_up, g_down)
        tallies[layer] = [*ups, *mlp, *att, *joined]
    ends = [(stash[0][s][0], d_mid[s], *sent[s]) for s in streams]
    input_grad, first = last_back(where, ends, vec)
    input_grad = input_grad[None]

    if fast:
        tiny = call(
            functools.partial(pack_body, n, heads, size),
            [((n, 24, 2 * rows), f32)],
            [where, first, *tallies[1], *tallies[0]],
            0,
            smem=1,
        )[0]
        tiny = scatter(tiny.reshape(n * 24, 2 * rows), where, f, n)
        tiny = (tiny[0] + tiny[1]) + (tiny[2] + tiny[3])
        tiny = tiny + core_swap(tiny)
        tiny = tiny + y_swap(tiny)
        vecs = pick(tiny[:16].reshape(8, LAYERS, 2, rows), 2, c)
        ups = pick(tiny[16:].reshape(LAYERS, 2, 2 * 2 * rows), 1, c)
        outs = None
        for layer in reversed(range(LAYERS)):
            g_qkv, g_proj, g_up, g_down = grads[layer]
            d = both_types(scatter(g_down, where, f, n))
            d = (d[0], y_swap(d[1]))
            u = scatter(g_up, where, f, n)
            u = to_rows(u, where)
            q = to_rows(scatter(g_qkv, where, f, n), where)
            p = both_types(scatter(g_proj, where, f, n, True))
            side = x_swap(p[1], n)
            p = both_types([p[0], side])
            p = (p[0], y_swap(p[1]))
            outs = finish(where, q, u, d, p, outs, layer, n, heads, size)
        qkv_out, proj_out, up_out, down_out = outs
    else:
        here = (jnp.arange(4) == quarter).reshape(1, 1, 4, 1)
        at_c = (jnp.arange(2) == c).reshape(1, 2, 1, 1)
        at_y = (jnp.arange(2) == y).reshape(1, 1, 2, 1)

        def rows_of(pair, i):
            return jnp.sum(pair[0][8 * i : 8 * i + 8] + pair[1][8 * i : 8 * i + 8], axis=0)

        by_owner = []
        for layer in range(LAYERS):
            tally = tallies[layer]
            ups, mlp, att, joined = [tally[2 * i : 2 * i + 2] for i in range(4)]
            if layer == 0:
                one_sums = [jnp.sum(first[8 * i : 8 * i + 8], axis=0) for i in range(2)]
            else:
                one_sums = [rows_of(tallies[layer - 1][2:4], i) for i in range(2)]
            joined = rows_of(joined, 0).reshape(3, heads, 1, size)[0::2]
            joined = jnp.where(here, joined, 0.0).reshape(2, width)
            alike = [rows_of(mlp, 2), *one_sums, rows_of(att, 2), rows_of(att, 0), rows_of(att, 1)]
            alike = [0.25 * v for v in alike]
            vecs = [alike[1], alike[2], joined[0], joined[1], alike[3], alike[4], alike[5], alike[0]]
            vecs = jnp.stack(vecs).reshape(8, 2 * n, rows).transpose(1, 0, 2)
            up = rows_of(ups, 0).reshape(n, 1, 1, hid_rows // 2)
            up = jnp.where(at_c & at_y, up, 0.0).reshape(2 * n, hid_rows)
            by_owner.append(jnp.concatenate([vecs.reshape(2 * n, 8 * rows), up], axis=1))
        total = lax.psum(jnp.stack(by_owner, axis=1), ("fsdp", "seq", "replica"))
        tiny = pick(total, 0, 2 * f + c)
        vecs = tiny[:, : 8 * rows].reshape(LAYERS, 8, rows).transpose(1, 0, 2)
        ups = tiny[:, 8 * rows :]
        axes = ("replica", "seq")

        def owned(full):
            block = lax.psum_scatter(full, "fsdp", scatter_dimension=0, tiled=True)
            half = block.shape[0] // 2
            return widen(lax.dynamic_slice_in_dim(block, c * half, half, axis=0))

        outs = []
        for layer in range(LAYERS):
            g_qkv, g_proj, g_up, g_down = grads[layer]
            g = lax.all_gather(g_qkv, axes, axis=0).reshape(4, width, 3, heads, size)
            qkv_out = owned(g.transpose(1, 2, 3, 0, 4).reshape(width, 3 * width))
            g = lax.all_gather(g_proj, axes, axis=0).reshape(4, heads, size, width)
            proj_out = owned(g.transpose(1, 0, 2, 3).reshape(width, width))
            g = lax.all_gather(g_up, axes, axis=0)
            g = g.reshape(2, 2, width, n, hid_rows // 2)
            up_out = owned(g.transpose(2, 3, 1, 0, 4).reshape(width, hidden))
            g = lax.all_gather(g_down, axes, axis=0)
            g = g.reshape(2, 2, n, hid_rows // 2, width)
            down_out = owned(g.transpose(2, 1, 0, 3, 4).reshape(hidden, width))
            outs.append((qkv_out, proj_out, up_out, down_out))
        qkv_out, proj_out, up_out, down_out = [
            jnp.stack([outs[layer][i] for layer in range(LAYERS)]) for i in range(4)
        ]
    return (
        clips_out,
        input_grad,
        vecs[GAIN_ONE],
        vecs[SHIFT_ONE],
        qkv_out,
        vecs[QUERY_B],
        vecs[VALUE_B],
        proj_out,
        vecs[PROJ_B],
        vecs[GAIN_TWO],
        vecs[SHIFT_TWO],
        up_out,
        ups,
        down_out,
        vecs[DOWN_B],
    )


def solution(mesh):
    tokens = P(("fsdp", "replica"), "seq", None)
    vector = P(None, ("fsdp", "seq"))
    matrix = P(None, ("fsdp", "seq"), None)
    kinds = [
        vector,
        vector,
        matrix,
        vector,
        vector,
        matrix,
        vector,
        vector,
        vector,
        matrix,
        vector,
        matrix,
        vector,
    ]
    return jax.shard_map(
        functools.partial(on_device, n=mesh.shape["fsdp"]),
        mesh=mesh,
        in_specs=(tokens, tokens, P(("fsdp", "replica")), *kinds),
        out_specs=(tokens, tokens, *kinds),
        check_vma=False,
    )
```

```python
import functools

import jax
import jax.numpy as jnp
from jax import lax
from jax.experimental import pallas as pl
from jax.experimental.pallas import tpu as pltpu
from jax.sharding import PartitionSpec as P


HEADS = 16
LAYERS = 2
norm_eps = 1e-06
bf16 = jnp.bfloat16
f32 = jnp.float32


def widen(array):
    return array.astype(f32)


def dot(a, b, dims):
    return lax.dot_general(a, b, (dims, ((), ())), preferred_element_type=f32)


def mm(a, b):
    return dot(a, b, ((1,), (0,)))


def mm_t(a, b):
    return dot(a, b, ((1,), (1,)))


def t_mm(a, b):
    return dot(a, b, ((0,), (0,)))


PAIR = [(0, 1), (1, 0)]


def core_swap(v):
    return lax.ppermute(v, "seq", PAIR)


def y_swap(v):
    return lax.ppermute(v, "replica", PAIR)


def x_swap(v, n):
    return lax.ppermute(v, "fsdp", [(f, f ^ 1) for f in range(n)])


def z_from(v, k, n):
    nz = n // 2
    return lax.ppermute(
        v, "fsdp", [(((z + k) % nz) * 2 + x, z * 2 + x) for z in range(nz) for x in range(2)]
    )


def pick(array, axis, at):
    return lax.dynamic_index_in_dim(array, at, axis, keepdims=False)


TILE = 224
COLS = 256
VMEM_LIMIT = 20 * 1024 * 1024
HBM = pltpu.MemorySpace.HBM


def call(body, outs, args, flops, transcendentals=0, scratch=(), smem=0):
    shapes = tuple(jax.ShapeDtypeStruct(o[0], o[1]) for o in outs)
    far = [i for i, o in enumerate(outs) if len(o) > 2 and o[2]]
    n_in, n_out, n_far = len(args), len(outs), len(far)

    def run(*refs):
        out_refs = list(refs[n_in : n_in + n_out])
        rest = refs[n_in + n_out :]
        sems = rest[-1] if far else None
        copies = {}
        for j, i in enumerate(far):
            copies[i] = pltpu.make_async_copy(rest[j], out_refs[i], sems.at[j])
            out_refs[i] = rest[j]
        extra = rest[n_far:-1] if far else rest[n_far:]
        body(lambda i: copies[i].start(), *refs[:n_in], *out_refs, *extra)
        for copy in copies.values():
            copy.wait()

    touched = sum(a.size * a.dtype.itemsize for a in (*args, *shapes))
    scratch = [pltpu.VMEM(*outs[i][:2]) for i in far] + list(scratch)
    if far:
        scratch.append(pltpu.SemaphoreType.DMA((n_far,)))
    spaces = [pltpu.SMEM if i < smem else pltpu.VMEM for i in range(n_in)]
    return pl.pallas_call(
        run,
        out_shape=shapes,
        in_specs=[pl.BlockSpec(memory_space=s) for s in spaces],
        out_specs=tuple(
            pl.BlockSpec(memory_space=HBM if i in far else pltpu.VMEM) for i in range(n_out)
        ),
        scratch_shapes=scratch,
        compiler_params=pltpu.CompilerParams(vmem_limit_bytes=VMEM_LIMIT),
        cost_estimate=pl.CostEstimate(
            flops=flops, bytes_accessed=touched, transcendentals=transcendentals
        ),
    )(*args)


def norm_parts(inputs):
    center = inputs - jnp.mean(inputs, axis=-1, keepdims=True)
    spread = jnp.mean(center * center, axis=-1, keepdims=True)
    scale = lax.rsqrt(spread + norm_eps)
    return center * scale, scale


def norm_grad(e, inputs, gain):
    unit, scale = norm_parts(inputs)
    eg = e * gain
    d = scale * (
        eg
        - jnp.mean(eg, axis=-1, keepdims=True)
        - unit * jnp.mean(eg * unit, axis=-1, keepdims=True)
    )
    return d, e * unit


def eight(v):
    return jnp.sum(v.reshape(v.shape[0] // 8, 8, v.shape[1]), axis=0)


def one(v):
    return jnp.sum(v, axis=0, keepdims=True)


def by_rows(half_rows, step):
    for half in range(2):

        @pl.loop(0, half_rows // TILE)
        def _(i):
            start = pl.multiple_of(i * TILE, TILE)
            step(pl.ds(half * half_rows + start, TILE), half, pl.ds(start, TILE))


def by_cols(width, step):
    @pl.loop(0, width // COLS)
    def _(i):
        step(pl.ds(pl.multiple_of(i * COLS, COLS), COLS))


def summed(sent, half, part):
    return sum(widen(sent[2 * i + half][part, :]) for i in range(3))


def put(ref, cols, value):
    ref[:, cols] = value.astype(ref.dtype)


def put_halves(refs, cols, value):
    rows = refs[0].shape[0]
    for i, ref in enumerate(refs):
        ref[:, cols] = value[i * rows : (i + 1) * rows].astype(ref.dtype)


def heads_of(ref, width, size, h):
    return [ref[:, i * width + h * size : i * width + (h + 1) * size] for i in range(3)]


GAIN_ONE, SHIFT_ONE, QUERY_B, VALUE_B, PROJ_B, GAIN_TWO, SHIFT_TWO, DOWN_B = range(8)


def row(vec, which, layer):
    at = 2 * which + layer
    return vec[at : at + 1, :]


def attend_body(layer, heads, size, flush, *refs):
    if layer == 0:
        base, vec, w_qkv, fix, w_proj = refs[:5]
        normed, qkv, attended, stat = refs[5:9]
        sent, shift = None, 0
    else:
        base, sent, (vec, w_qkv, fix, w_proj) = refs[0], refs[1:7], refs[7:11]
        resid, normed, qkv, attended, stat = refs[11:16]
        shift = 1
    low = refs[-2:]
    width = heads * size

    def norm(whole, half, part_rows):
        value = widen(base[whole, :])
        if sent is not None:
            value = value + (summed(sent, half, part_rows) + row(vec, DOWN_B, layer - 1))
            resid[whole, :] = value
        unit, _ = norm_parts(value)
        normed[whole, :] = (
            unit * row(vec, GAIN_ONE, layer) + row(vec, SHIFT_ONE, layer)
        ).astype(bf16)

    by_rows(base.shape[0] // 2, norm)
    for i in range(shift + 1):
        flush(i)

    def project(cols):
        value = mm(normed[...], w_qkv[:, cols]) + fix[2 * layer : 2 * layer + 1, cols]
        qkv[:, cols] = (value * fix[2 * layer + 1 : 2 * layer + 2, cols]).astype(bf16)

    by_cols(3 * width, project)
    flush(shift + 1)
    for h in range(heads):
        q, k, v = heads_of(qkv, width, size, h)
        s = mm_t(q, k)
        peak = jnp.max(s, axis=-1, keepdims=True)
        e = jnp.exp(s - peak)
        total = jnp.sum(e, axis=-1, keepdims=True)
        value = mm(e.astype(bf16), v) * (1.0 / total)
        attended[:, h * size : (h + 1) * size] = value.astype(bf16)
        stat[:, h : h + 1] = peak + jnp.log(total)
    flush(shift + 2)
    flush(shift + 3)
    by_cols(base.shape[1], lambda cols: put_halves(low, cols, mm(attended[...], w_proj[:, cols])))


def attend(base, sent, vec, w_qkv, fix, w_proj, layer, heads, size):
    toks, width = base.shape
    outs = [((toks, width), bf16, True), ((toks, 3 * heads * size), bf16, True)]
    outs = outs + [((toks, heads * size), bf16, True), ((toks, 128), f32, True)]
    outs = outs + [((toks // 2, width), bf16)] * 2
    if layer:
        outs = [((toks, width), f32, True)] + outs
    args = [base, *(sent or ()), vec, w_qkv, fix, w_proj]
    flops = 8 * toks * width * heads * size + 4 * heads * toks * toks * size
    body = functools.partial(attend_body, layer, heads, size)
    got = call(body, outs, args, flops, heads * toks * toks)
    return got if layer else (base, *got)


ROOT_HALF = 0.7071067811865476
ROOT_TWO_PI_INV = 0.3989422804014327


def up_body(layer, flush, base, *refs):
    sent, (vec, w_up, up_b, mid, normed, active, slope) = refs[:6], refs[6:]

    def norm(whole, half, part_rows):
        value = widen(base[whole, :])
        value = value + (
            summed(sent, half, part_rows) + row(vec, PROJ_B, layer)
        )
        mid[whole, :] = value
        unit, _ = norm_parts(value)
        normed[whole, :] = (
            unit * row(vec, GAIN_TWO, layer) + row(vec, SHIFT_TWO, layer)
        ).astype(bf16)

    by_rows(base.shape[0] // 2, norm)
    flush(0)
    flush(1)

    def up(cols):
        pre = mm(normed[...], w_up[:, cols]) + up_b[layer : layer + 1, cols]
        half = 0.5 * (1.0 + lax.erf(pre * ROOT_HALF))
        put(active, cols, pre * half)
        put(slope, cols, half + pre * (ROOT_TWO_PI_INV * jnp.exp(-0.5 * pre * pre)))

    by_cols(w_up.shape[1], up)
    flush(2)
    flush(3)


def go_up(base, sent, vec, w_up, up_b, layer):
    toks, width = base.shape
    hid = w_up.shape[1]
    outs = [((toks, width), f32, True), ((toks, width), bf16, True)]
    outs = outs + [((toks, hid), bf16, True), ((toks, hid), bf16, True)]
    args = [base, *sent, vec, w_up, up_b]
    body = functools.partial(up_body, layer)
    return call(body, outs, args, 2 * toks * width * hid, toks * hid)


def down_body(flush, active, w_down, *low):
    by_cols(
        w_down.shape[1], lambda cols: put_halves(low, cols, mm(active[...], w_down[:, cols]))
    )


def go_down(active, w_down):
    outs = [((active.shape[0] // 2, w_down.shape[1]), bf16)] * 2
    flops = 2 * active.size * w_down.shape[1]
    return call(down_body, outs, [active, w_down], flops)


def mlp_back_tail(flush, at, d_mlp, slope, w_down, w_up, d_pre, low, up_sum):
    def back(cols):
        value = (mm_t(d_mlp[...], w_down[cols, :]) * widen(slope[:, cols])).astype(bf16)
        d_pre[:, cols] = value
        up_sum[:, cols] = eight(widen(value))

    by_cols(w_down.shape[0], back)
    flush(at)
    by_cols(w_up.shape[0], lambda cols: put_halves(low, cols, mm_t(d_pre[...], w_up[cols, :])))


def mlp_back_first(flush, d_mlp, slope, w_down, w_up, d_pre, near, far, up_sum, sums):
    sums[...] = jnp.zeros_like(sums)

    def count(whole, half, part_rows):
        sums[16:24, :] += eight(widen(d_mlp[whole, :]))

    by_rows(d_mlp.shape[0] // 2, count)
    mlp_back_tail(flush, 0, d_mlp, slope, w_down, w_up, d_pre, (near, far), up_sum)


def mlp_back_body(layer, flush, base, d_mid, *refs):
    sent, (vec, slope, w_down, w_up) = refs[:6], refs[6:10]
    grad, d_mlp, d_pre, near, far, up_sum, sums = refs[10:]
    sums[...] = jnp.zeros_like(sums)

    def norm(whole, half, part_rows):
        e = summed(sent, half, part_rows)
        d, by_gain = norm_grad(e, widen(base[whole, :]), row(vec, GAIN_ONE, layer + 1))
        value = d_mid[whole, :] + d
        grad[whole, :] = value
        low_value = value.astype(bf16)
        d_mlp[whole, :] = low_value
        sums[0:8, :] += eight(by_gain)
        sums[8:16, :] += eight(e)
        sums[16:24, :] += eight(widen(low_value))

    by_rows(base.shape[0] // 2, norm)
    flush(0)
    flush(1)
    mlp_back_tail(flush, 2, d_mlp, slope, w_down, w_up, d_pre, (near, far), up_sum)


def mlp_back(first, base, d_mid, sent, vec, slope, w_down, w_up, layer):
    toks, hid = slope.shape
    width = w_up.shape[0]
    outs = [((toks, hid), bf16, True)] + [((toks // 2, width), bf16)] * 2
    outs = outs + [((8, hid), f32), ((24, width), f32)]
    flops = 4 * toks * hid * width
    if first is not None:
        return call(mlp_back_first, outs, [first, slope, w_down, w_up], flops)
    outs = [((toks, width), f32, True), ((toks, width), bf16, True), *outs]
    args = [base, d_mid, *sent, vec, slope, w_down, w_up]
    return call(functools.partial(mlp_back_body, layer), outs, args, flops)


def attend_back_body(layer, heads, size, flush, *refs):
    grad, mid, sent, (vec, qkv, stat, w_proj, w_qkv) = *refs[:2], refs[2:8], refs[8:13]
    d_mid, d_branch, d_joined, near, far, sums, joined_sum, d_att = refs[13:]
    width = heads * size
    sums[...] = jnp.zeros_like(sums)

    def norm(whole, half, part_rows):
        e = summed(sent, half, part_rows)
        d, by_gain = norm_grad(e, mid[whole, :], row(vec, GAIN_TWO, layer))
        value = widen(grad[whole, :]) + d
        d_mid[whole, :] = value
        low_value = value.astype(bf16)
        d_branch[whole, :] = low_value
        sums[0:8, :] += eight(by_gain)
        sums[8:16, :] += eight(e)
        sums[16:24, :] += eight(widen(low_value))

    by_rows(mid.shape[0] // 2, norm)
    flush(0)
    flush(1)
    d_att[...] = mm_t(d_branch[...], w_proj[...]).astype(bf16)
    rows = stat[...].T
    for h in range(heads):
        q, k, v = heads_of(qkv, width, size, h)
        d = d_att[:, h * size : (h + 1) * size]
        p = jnp.exp(mm_t(k, q) - rows[h : h + 1, :])
        dv = mm(p.astype(bf16), d)
        d_p = mm_t(v, d)
        ds = (p * (d_p - jnp.sum(p * d_p, axis=0, keepdims=True))).astype(bf16)
        dk = mm(ds, q)
        dq = widen(t_mm(ds, k).astype(bf16)) * 0.125
        for i, value in enumerate((dq, dk, dv)):
            at = i * width + h * size
            d_joined[:, at : at + size] = value.astype(bf16)
    flush(2)
    joined_sum[...] = eight(widen(d_joined[...]))
    by_cols(
        w_qkv.shape[0],
        lambda cols: put_halves((near, far), cols, mm_t(d_joined[...], w_qkv[cols, :])),
    )


def attend_back(grad, mid, sent, vec, qkv, stat, w_proj, w_qkv, layer, heads, size):
    toks, width = mid.shape
    wide = 3 * heads * size
    outs = [((toks, width), f32, True), ((toks, width), bf16, True), ((toks, wide), bf16, True)]
    outs = outs + [((toks // 2, width), bf16)] * 2 + [((24, width), f32), ((8, wide), f32)]
    args = [grad, mid, *sent, vec, qkv, stat, w_proj, w_qkv]
    flops = 8 * toks * width * heads * size + 10 * heads * toks * toks * size
    return call(
        functools.partial(attend_back_body, layer, heads, size),
        outs,
        args,
        flops,
        heads * toks * toks,
        [pltpu.VMEM((toks, heads * size), bf16)],
    )


def last_body(flush, where, *refs):
    streams, vec, grad, sums = (refs[0:8], refs[8:16]), refs[16], refs[17], refs[18]
    sums[...] = jnp.zeros_like(sums)
    for s, (base, d_mid, *sent) in enumerate(streams):

        def norm(whole, half, part_rows):
            e = summed(sent, half, part_rows)
            d, by_gain = norm_grad(e, widen(base[whole, :]), row(vec, GAIN_ONE, 0))
            sums[0:8, :] += eight(by_gain)
            sums[8:16, :] += eight(e)
            if half == 0:

                @pl.when(where[1] == s)
                def _():
                    grad[part_rows, :] = d_mid[whole, :] + d

        by_rows(base.shape[0] // 2, norm)
    flush(0)


def last_back(where, streams, vec):
    toks, width = streams[0][0].shape
    outs = [((toks // 2, width), f32, True), ((16, width), f32)]
    args = [where, *streams[0], *streams[1], vec]
    return call(last_body, outs, args, 20 * toks * width, smem=1)


def pick_body(toks, flush, where, own, side, across, beside, *outs):
    for s, out in enumerate(outs):

        @pl.when(where[1] == s)
        def _():
            out[0:toks, :] = own[...]
            out[toks:, :] = side[...]

        @pl.when(where[1] != s)
        def _():
            out[0:toks, :] = across[...]
            out[toks:, :] = beside[...]

        flush(s)


def halves(first, second, c):
    low = lax.broadcasted_iota(jnp.int32, first.shape, 1) < first.shape[1] // 2
    half = first.shape[1] // 2
    zero = jnp.where(low, first, pltpu.roll(second, half, 1))
    other = jnp.where(low, pltpu.roll(first, half, 1), second)
    return jnp.where(c == 0, zero, other), jnp.where(c == 0, other, zero)


def units_q_body(rows, heads, size, flush, where, qkv, *refs):
    vectors, (q_mine, q_theirs, small, wide) = refs[:-4], refs[-4:]
    c, y = where[0], where[1]
    pair = 2 * size
    for i, vector in enumerate(vectors):
        for at in (0, size):
            wide[2 * i : 2 * i + 2, at : at + size] = widen(vector[...])
    small[...] = wide[...].astype(bf16)
    for layer in range(LAYERS):
        at = slice(layer * rows, (layer + 1) * rows)
        for t in range(3):
            for h in range(0, heads, 2):
                tiles = []
                for i in range(2):
                    start = ((t * heads + h + i) * 2 + y) * pair
                    tiles.append(widen(qkv[layer, :, pl.ds(pl.multiple_of(start, pair), pair)]))
                mine, theirs = halves(*tiles, c)
                cols = slice((t * heads + h) * size, (t * heads + h + 2) * size)
                q_mine[at, cols] = mine.astype(bf16)
                q_theirs[at, cols] = theirs.astype(bf16)
    q_theirs[2 * rows :, :] = jnp.zeros((16, q_theirs.shape[1]), bf16)
    q_theirs[2 * rows :, 0:pair] = wide[...].astype(bf16)


def units_u_body(rows, pair, flush, where, up, down, u_mine, u_theirs, d_unit):
    c, y = where[0], where[1]
    for layer in range(LAYERS):
        at = slice(layer * rows, (layer + 1) * rows)
        for f in range(up.shape[2] // (4 * pair)):
            for ref, core in ((u_mine, c), (u_theirs, 1 - c)):
                start = pl.multiple_of(f * 4 * pair + core * 2 * pair + y * pair, pair)
                ref[at, f * pair : (f + 1) * pair] = up[layer, :, pl.ds(start, pair)]
        half = down.shape[1] // 2
        d_unit[layer] = down[layer, pl.ds(pl.multiple_of(y * half, half), half), :]


def join_q_body(rows, flush, where, q_mine, q_side, small, up_b, q0, q1):
    c, y = where[0], where[1]
    pair = small.shape[1]
    for layer, q in enumerate((q0, q1)):
        join_rows(c, rows, q, layer, q_mine, q_side)
    low = lax.broadcasted_iota(jnp.int32, small.shape, 1) < pair // 2
    own, side = widen(small[...]), widen(q_side[2 * rows :, 0:pair])
    both = jnp.where(c == 0, jnp.where(low, own, side), jnp.where(low, side, own))
    q0[2 * rows :, :] = jnp.zeros((16, q0.shape[1]), bf16)
    q0[2 * rows :, 0:pair] = both.astype(bf16)
    ups = widen(up_b[...])
    ups = jnp.where(y == 0, ups[:, 0:pair], ups[:, pair : 2 * pair])
    q0[2 * rows :, pair : 2 * pair] = ups.astype(bf16)


def join_rows(c, rows, out, layer, mine, side):
    at = slice(layer * rows, (layer + 1) * rows)
    out[pl.ds(pl.multiple_of(c * rows, rows), rows), :] = mine[at, :]
    out[pl.ds(pl.multiple_of((1 - c) * rows, rows), rows), :] = side[at, :]


def join_u_body(rows, flush, where, u_mine, u_side, own, side, u0, u1, *outs):
    c, y, x = where[0], where[1], where[2]
    for layer, (u, out) in enumerate(zip((u0, u1), outs)):
        join_rows(c, rows, u, layer, u_mine, u_side)

        @pl.when(x == y)
        def _():
            out[...] = own[layer]

        @pl.when(x != y)
        def _():
            out[...] = side[layer]


def prep_body(n, heads, size, flush, where, small, vec, fix, up_b):
    c, y = where[0], where[1]
    pair = 2 * size
    for f in range(n):
        vec[:, f * pair : (f + 1) * pair] = widen(small[:, f * 2 * pair : f * 2 * pair + pair])
        up_b[:, f * pair : (f + 1) * pair] = widen(
            small[:, f * 2 * pair + pair : (f + 1) * 2 * pair]
        )
    width = heads * size
    for layer in range(LAYERS):
        for t, which in ((0, QUERY_B), (2, VALUE_B)):
            for i in range(0, heads, 2):
                tiles = [
                    widen(small[:, pl.ds(pl.multiple_of((2 * (i + j) + y) * 2 * pair, 2 * pair), pair)])
                    for j in range(2)
                ]
                mine, _ = halves(*tiles, c)
                at = 2 * which + layer
                start = t * width + i * size
                fix[2 * layer : 2 * layer + 1, start : start + pair] = mine[at : at + 1, :]
        fix[2 * layer : 2 * layer + 1, width : 2 * width] = jnp.zeros((1, width), f32)
        fix[2 * layer + 1 : 2 * layer + 2, 0:width] = jnp.full((1, width), 0.125, f32)
        fix[2 * layer + 1 : 2 * layer + 2, width:] = jnp.ones((1, 2 * width), f32)


def place_body(count, rows, extra, at_ref, *refs):
    n_out = 2 if extra else 1
    blocks, outs, sems = refs[: -1 - n_out], refs[-1 - n_out : -1], refs[-1]
    copies = []
    per = count // len(blocks)
    for i in range(count):
        source, base = blocks[i // per], (i % per) * (rows + extra)
        start = pl.multiple_of(at_ref[i] * rows, rows)
        copies.append(
            pltpu.make_async_copy(
                source.at[pl.ds(base, rows)], outs[0].at[pl.ds(start, rows)], sems.at[0, i]
            )
        )
        if extra:
            start = pl.multiple_of(at_ref[i] * 256, 256)
            copies.append(
                pltpu.make_async_copy(
                    source.at[pl.ds(base + rows, extra), pl.ds(0, 256)],
                    outs[1].at[:, pl.ds(start, 256)],
                    sems.at[1, i],
                )
            )
    for copy in copies:
        copy.start()
    for copy in copies:
        copy.wait()


def place(blocks, at, count, extra):
    total, cols = sum(b.shape[0] for b in blocks), blocks[0].shape[1]
    rows = total // count - extra
    outs = [jax.ShapeDtypeStruct((count * rows, cols), bf16)]
    if extra:
        outs.append(jax.ShapeDtypeStruct((extra, count * 256), bf16))
    return pl.pallas_call(
        functools.partial(place_body, count, rows, extra),
        in_specs=[pl.BlockSpec(memory_space=pltpu.SMEM)]
        + [pl.BlockSpec(memory_space=pltpu.VMEM)] * len(blocks),
        out_specs=tuple([pl.BlockSpec(memory_space=pl.ANY)] * len(outs)),
        scratch_shapes=[pltpu.SemaphoreType.DMA((2, count))],
        out_shape=tuple(outs),
        compiler_params=pltpu.CompilerParams(vmem_limit_bytes=VMEM_LIMIT),
        cost_estimate=pl.CostEstimate(flops=0, bytes_accessed=4 * total * cols, transcendentals=0),
    )(at, *blocks)


def z_pair(v, bit, n):
    return lax.ppermute(v, "fsdp", [(f, f ^ (2 * bit)) for f in range(n)])


def gather_first(unit, me, n, extra):
    nz = n // 2
    line = [unit] + [z_from(unit, k, n) for k in range(1, nz)]
    line = jnp.concatenate(line, axis=0)
    other = x_swap(line, n)
    z, x = me // 2, me % 2
    at = [((z + k) % nz) * 2 + x for k in range(nz)]
    at = at + [((z + k) % nz) * 2 + 1 - x for k in range(nz)]
    return place([line, other], jnp.stack(at).astype(jnp.int32), n, extra)


def along_z(unit, n):
    pair = z_pair(unit, 1, n)
    near = jnp.concatenate([unit, pair], axis=0)
    return near, z_pair(near, 2, n)


def gather_rows(unit, me, n):
    near, far = along_z(unit, n)
    near_x = x_swap(near, n)
    far_x = x_swap(far, n)
    z, x = me // 2, me % 2
    at = [(z ^ k) * 2 + x for k in range(4)] + [(z ^ k) * 2 + 1 - x for k in range(4)]
    at = jnp.stack(at).astype(jnp.int32)
    return place([near, far, near_x, far_x], at, n, 0)


def gather_line(unit, me, n):
    near, far = along_z(unit, n)
    at = jnp.stack([(me // 2) ^ k for k in range(4)]).astype(jnp.int32)
    return place([near, far], at, 4, 0)[0]


def split_body(nz, flush, where, *refs):
    grad, other = (refs[0], refs[1]) if len(refs) == 2 + nz else (refs[0], None)
    outs = refs[-nz:]
    x, z = where[2], where[3]
    rows = outs[0].shape[0]
    for k in range(nz):
        to = lax.rem(z - k + nz, nz)
        if other is None:
            value = grad[pl.ds(pl.multiple_of(to * rows, rows), rows), :]
        else:
            mine = grad[pl.ds(pl.multiple_of((to * 2 + x) * rows, rows), rows), :]
            value = widen(mine) + widen(other[pl.ds(pl.multiple_of(to * rows, rows), rows), :])
        outs[k][...] = value.astype(outs[k].dtype)


def scatter(grad, where, me, n, line=False):
    nz = n // 2
    count = nz if line else n
    rows, cols = grad.shape[0] // count, grad.shape[1]
    args = [where, grad]
    if not line:
        blocks = grad.reshape(nz, 2, rows, cols)
        sent = pick(blocks, 1, 1 - me % 2).reshape(nz * rows, cols)
        args.append(x_swap(sent, n))
    outs = [((rows, cols), f32)] + [((rows, cols), grad.dtype)] * (nz - 1)
    got = call(functools.partial(split_body, nz), outs, args, grad.size, smem=1)
    return [got[0]] + [z_from(got[k], k, n) for k in range(1, nz)]


def total_of(refs):
    total = widen(refs[0][...])
    for ref in refs[1:]:
        total = total + widen(ref[...])
    return total


def rows_body(rows, flush, where, *refs):
    mine, sent, total = refs[-3:]
    value = refs[0][...]
    for ref in refs[1:-3]:
        value = value + widen(ref[ref.shape[0] - 2 * rows :, :])
    total[...] = value
    c = where[0]
    mine[...] = total[pl.ds(pl.multiple_of(c * rows, rows), rows), :]
    sent[0:rows, :] = mine[...].astype(bf16)
    other = total[pl.ds(pl.multiple_of((1 - c) * rows, rows), rows), :]
    sent[rows:, :] = other.astype(bf16)


def to_rows(pieces, where):
    rows, cols = pieces[0].shape[0] // 2, pieces[0].shape[1]
    outs = [((rows, cols), f32), ((2 * rows, cols), bf16)]
    mine, sent = call(
        functools.partial(rows_body, rows),
        outs,
        [where, *pieces],
        4 * sent_size(pieces),
        scratch=[pltpu.VMEM((2 * rows, cols), f32)],
        smem=1,
    )
    across = y_swap(sent)
    side = core_swap(sent[rows:])
    beyond = core_swap(across[rows:])
    return mine, side, across, beyond


def sent_size(pieces):
    return sum(p.size for p in pieces)


def sum_body(flush, *refs):
    total = total_of(refs[:-2])
    refs[-2][...] = total
    refs[-1][...] = total.astype(refs[-1].dtype)


def both_types(pieces):
    shape = pieces[0].shape
    return call(sum_body, [(shape, f32), (shape, bf16)], list(pieces), sent_size(pieces))


def finish_body(layer, n, heads, size, first, where, *refs):
    q, u = refs[0:4], refs[4:8]
    d_own, d_side, p_own, p_side = refs[8:12]
    outs = refs[12 if first else 16 :][:4]
    b_q, b_p, b_u, b_d, sems = refs[-5:]
    c, y, x = where[0], where[1], where[2]
    pair = 2 * size
    rows = q[0].shape[0]

    def quarters(pieces, cols):
        mine, side = pieces[0][:, cols], widen(pieces[1][:, cols])
        across, beyond = widen(pieces[2][0:rows, cols]), widen(pieces[3][:, cols])
        here = (jnp.where(c == 0, mine, side), jnp.where(c == 0, side, mine))
        there = (jnp.where(c == 0, across, beyond), jnp.where(c == 0, beyond, across))
        return [
            [jnp.where(y == at, here[core], there[core]) for core in range(2)] for at in range(2)
        ]

    def out(i, buffer):
        return pltpu.make_async_copy(buffer, outs[i].at[layer], sems.at[i])

    for t in range(3):
        for h in range(0, heads, 2):
            at = (t * heads + h) * size
            got = quarters(q, slice(at, at + pair))
            for across in range(2):
                one_head, next_head = halves(*got[across], 0)
                start = (t * heads + h) * 2 * pair + across * pair
                b_q[:, start : start + pair] = one_head
                b_q[:, start + 2 * pair : start + 3 * pair] = next_head
    out(0, b_q).start()
    for f in range(n):
        got = quarters(u, slice(f * pair, (f + 1) * pair))
        for across in range(2):
            for core in range(2):
                start = f * 4 * pair + core * 2 * pair + across * pair
                b_u[:, start : start + pair] = got[across][core]
    out(2, b_u).start()
    half = d_own.shape[0]
    b_d[pl.ds(pl.multiple_of(y * half, half), half), :] = d_own[...]
    b_d[pl.ds(pl.multiple_of((1 - y) * half, half), half), :] = widen(d_side[...])
    out(3, b_d).start()
    b_p[...] = jnp.where(x == y, p_own[...], widen(p_side[...]))
    out(1, b_p).start()
    for i, buffer in enumerate((b_q, b_p, b_u, b_d)):
        out(i, buffer).wait()


def finish(where, q, u, d, p, past, layer, n, heads, size):
    rows = q[0].shape[0]
    width = HEADS * size
    hid = n * 8 * size
    shapes = [(rows, 3 * width), (rows, width), (rows, hid), (2 * d[0].shape[0], width)]
    args = [where, *q, *u, *d, *p]
    aliases = {}
    if past is not None:
        aliases = {len(args) + i: i for i in range(4)}
        args = args + list(past)
    first = past is None
    spaces = [pltpu.SMEM] + [pltpu.VMEM] * 12 + [HBM] * (0 if first else 4)
    return pl.pallas_call(
        functools.partial(finish_body, layer, n, heads, size, first),
        out_shape=tuple(jax.ShapeDtypeStruct((LAYERS, *s), f32) for s in shapes),
        in_specs=[pl.BlockSpec(memory_space=s) for s in spaces],
        out_specs=tuple([pl.BlockSpec(memory_space=HBM)] * 4),
        scratch_shapes=[pltpu.VMEM(s, f32) for s in shapes]
        + [pltpu.SemaphoreType.DMA((4,))],
        input_output_aliases=aliases,
        compiler_params=pltpu.CompilerParams(vmem_limit_bytes=VMEM_LIMIT),
        cost_estimate=pl.CostEstimate(
            flops=0, bytes_accessed=4 << 20, transcendentals=0
        ),
    )(*args)


def pack_body(n, heads, size, flush, where, *refs):
    first, upper, lower, out = refs[0], refs[1:9], refs[9:17], refs[17]
    c, y = where[0], where[1]
    pair = 2 * size
    out[...] = jnp.zeros_like(out)

    def rows_of(ref, i):
        return one(ref[8 * i : 8 * i + 8, :])

    def put_vector(which, layer, value):
        at = 2 * which + layer
        for f in range(n):
            out[f, at : at + 1, :] = 0.25 * value[:, f * pair : (f + 1) * pair]

    def both(refs_of, i):
        return rows_of(refs_of[0], i) + rows_of(refs_of[1], i)

    for layer, group in ((1, upper), (0, lower)):
        ups, mlp, att, joined = group[0:2], group[2:4], group[4:6], group[6:8]
        put_vector(DOWN_B, layer, both(mlp, 2))
        put_vector(GAIN_TWO, layer, both(att, 0))
        put_vector(SHIFT_TWO, layer, both(att, 1))
        put_vector(PROJ_B, layer, both(att, 2))
        value = one(ups[0][...]) + one(ups[1][...])
        at = 16 + 4 * layer + 2 * c + y
        for f in range(n):
            out[f, pl.ds(at, 1), :] = value[:, f * pair : (f + 1) * pair]
        value = one(joined[0][...]) + one(joined[1][...])
        low = lax.broadcasted_iota(jnp.int32, (1, pair), 1) < size
        for t, which in ((0, QUERY_B), (2, VALUE_B)):
            at = 2 * which + layer
            for i in range(0, heads, 2):
                start = (t * heads + i) * size
                tile = value[:, start : start + pair]
                turned = pltpu.roll(jnp.broadcast_to(tile, (8, pair)), size, 1)[0:1, :]
                zero = jnp.zeros_like(tile)
                even = jnp.where(c == 0, jnp.where(low, tile, zero), jnp.where(low, zero, turned))
                odd = jnp.where(c == 0, jnp.where(low, turned, zero), jnp.where(low, zero, tile))
                out[2 * i + y, at : at + 1, :] = even
                out[2 * (i + 1) + y, at : at + 1, :] = odd
    mlp = lower[2:4]
    put_vector(GAIN_ONE, 1, both(mlp, 0))
    put_vector(SHIFT_ONE, 1, both(mlp, 1))
    put_vector(GAIN_ONE, 0, rows_of(first, 0))
    put_vector(SHIFT_ONE, 0, rows_of(first, 1))


def send_part(near, far):
    near_side, far_side = core_swap(far), core_swap(near)
    mine = (widen(near) + widen(near_side)).astype(bf16)
    across = y_swap(mine)
    beside = core_swap(across)
    return near, far, near_side, far_side, across, beside


def on_device(
    clips_in,
    cotangent,
    clip_mask,
    norm1_gain,
    norm1_bias,
    qkv_weight,
    query_bias,
    value_bias,
    proj_weight,
    proj_bias,
    norm2_gain,
    norm2_bias,
    up_weight,
    up_bias,
    down_weight,
    down_bias,
    *,
    n,
):
    c, y, f = lax.axis_index("seq"), lax.axis_index("replica"), lax.axis_index("fsdp")
    quarter = 2 * y + c
    toks, width = clips_in.shape[1], clips_in.shape[2]
    rows = qkv_weight.shape[1]
    hid_rows = down_weight.shape[1]
    hidden = up_weight.shape[2]
    size = width // HEADS
    heads = HEADS // 4
    fast = n == 8 and rows == size and hid_rows == 4 * rows

    where = jnp.stack([c, y, f % 2, f // 2]).astype(jnp.int32)

    def pair_tokens(own):
        across = y_swap(own)
        side, beside = core_swap(own), core_swap(across)
        return call(
            functools.partial(pick_body, toks),
            [((2 * toks, width), bf16, True)] * 2,
            [where, own, side, across, beside],
            0,
            smem=1,
        )

    resid = list(pair_tokens(clips_in[0]))
    masked = (widen(cotangent[0]) * widen(clip_mask)[0]).astype(bf16)
    start = pair_tokens(masked)

    def qkv_cols(w, at):
        w = w.reshape(*w.shape[:-1], 3, heads, 4, size)
        return pick(w, w.ndim - 2, at).reshape(*w.shape[:-4], 3 * heads * size)

    def up_cols(w, at_c, at_y):
        w = w.reshape(*w.shape[:-1], n, 2, 2, hid_rows // 2)
        w = pick(w, w.ndim - 2, at_y)
        return pick(w, w.ndim - 2, at_c).reshape(*w.shape[:-3], hidden // 4)

    flat = [
        norm1_gain,
        norm1_bias,
        query_bias,
        value_bias,
        proj_bias,
        norm2_gain,
        norm2_bias,
        down_bias,
    ]
    weights = []
    if fast:
        up_b_rows = jnp.concatenate([up_bias, jnp.zeros((14, hid_rows), bf16)], axis=0)
        wide = 3 * heads * size
        outs = [((2 * rows, wide), bf16), ((2 * rows + 16, wide), bf16)]
        q_mine, q_theirs, small = call(
            functools.partial(units_q_body, rows, heads, size),
            [*outs, ((16, 2 * size), bf16)],
            [where, qkv_weight, *flat],
            0,
            scratch=[pltpu.VMEM((16, 2 * size), f32)],
            smem=1,
        )
        q_side = core_swap(q_theirs)
        q0, q1 = call(
            functools.partial(join_q_body, rows),
            [((2 * rows + 16, wide), bf16), ((2 * rows, wide), bf16)],
            [where, q_mine, q_side, small, up_b_rows],
            0,
            smem=1,
        )
        outs = [((2 * rows, hidden // 4), bf16)] * 2
        u_mine, u_theirs, down_units = call(
            functools.partial(units_u_body, rows, 2 * size),
            [*outs, ((LAYERS, hid_rows // 2, width), bf16)],
            [where, up_weight, down_weight],
            0,
            smem=1,
        )
        p_side = x_swap(proj_weight, n)
        u0, u1, p0, p1 = call(
            functools.partial(join_u_body, rows),
            [*outs, *[((rows, width), bf16)] * 2],
            [where, u_mine, core_swap(u_theirs), proj_weight, p_side],
            0,
            smem=1,
        )
        for layer, (q, u, p) in enumerate(((q0, u0, p0), (q1, u1, p1))):
            if layer:
                got = gather_rows(q, f, n)
            else:
                got = gather_first(q, f, n, 16)
                shapes = [((16, width), f32), ((2 * LAYERS, wide), f32), ((16, hidden // 4), f32)]
                vec, fix, up_b = call(
                    functools.partial(prep_body, n, heads, size), shapes, [where, got[1]], 0, smem=1
                )
            weights.append(
                (
                    got[0],
                    gather_line(p, f, n),
                    gather_rows(u, f, n)[0],
                    gather_rows(down_units[layer], f, n)[0],
                )
            )
    else:
        packed = jnp.concatenate(flat + [up_bias], axis=1)
        everything = lax.all_gather(packed, ("fsdp", "seq"), axis=0)
        for layer in range(LAYERS):
            full = [
                lax.all_gather(w[layer], ("fsdp", "seq"), axis=0, tiled=True)
                for w in (qkv_weight, proj_weight, up_weight, down_weight)
            ]
            by_head = full[1].reshape(heads, 4, size, width)
            by_hid = full[3].reshape(n, 2, 2, hid_rows // 2, width)
            weights.append(
                (
                    qkv_cols(full[0], quarter),
                    pick(by_head, 1, quarter).reshape(heads * size, width),
                    up_cols(full[2], c, y),
                    pick(pick(by_hid, 2, y), 1, c).reshape(hidden // 4, width),
                )
            )

        vectors = everything[:, :, : 8 * rows].reshape(2 * n, LAYERS, 8, rows)
        vectors = widen(vectors.transpose(2, 1, 0, 3).reshape(8, LAYERS, width))
        vec = vectors.reshape(8 * LAYERS, width)
        up_b = everything[:, :, 8 * rows :].reshape(n, 2, LAYERS, 2, hid_rows // 2)
        up_b = pick(pick(up_b, 3, y), 1, c).transpose(1, 0, 2)
        up_b = widen(up_b.reshape(LAYERS, hidden // 4))
        by_head = vectors.reshape(8, LAYERS, heads, 4, size)
        by_head = pick(by_head, 3, quarter).reshape(8, LAYERS, heads * size)
        zero = jnp.zeros_like(by_head[0])
        add = jnp.concatenate([by_head[QUERY_B], zero, by_head[VALUE_B]], axis=1)
        times = jnp.concatenate([zero + 0.125, zero + 1.0, zero + 1.0], axis=1)
        fix = jnp.stack([add, times], axis=1).reshape(2 * LAYERS, -1)

    streams = range(2)
    sent = [None, None]
    stash = []
    for layer in range(LAYERS):
        w_qkv, w_proj, w_up, w_down = weights[layer]
        kept = []
        for s in streams:
            before, normed, qkv, attended, stat, *low = attend(
                resid[s], sent[s], vec, w_qkv, fix, w_proj, layer, heads, size
            )
            got = send_part(*low)
            mid, normed_two, active, slope = go_up(before, got, vec, w_up, up_b, layer)
            kept.append((before, normed, qkv, attended, mid, normed_two, slope, active, stat))
            sent[s] = send_part(*go_down(active, w_down))
            resid[s] = mid
        stash.append(kept)

    def own_rows(pair):
        return jnp.where(y == 0, pair[0], pair[1])

    last_bias = vec[2 * DOWN_B + LAYERS - 1]
    clips_out = own_rows([r[:toks] for r in resid]) + (
        widen(own_rows([p[0] for p in sent]))
        + widen(own_rows([p[2] for p in sent]))
        + widen(own_rows([p[4] for p in sent]))
        + last_bias
    )
    clips_out = clips_out.astype(bf16)[None]

    grads = [None] * LAYERS
    tallies = [None] * LAYERS
    d_mid, sent = [None, None], [None, None]

    def both_t_mm(left, right):
        return t_mm(
            jnp.concatenate(left, axis=0), jnp.concatenate(right, axis=0)
        ).astype(bf16)

    for layer in reversed(range(LAYERS)):
        w_qkv, w_proj, w_up, w_down = weights[layer]
        kept = stash[layer]
        d_mlp, d_pre, d_branch, d_joined, grad = [], [], [], [], []
        ups, mlp, att, joined = [], [], [], []
        for s in streams:
            slope = kept[s][6]
            if layer == LAYERS - 1:
                got = (start[s], start[s]) + tuple(
                    mlp_back(start[s], None, None, None, None, slope, w_down, w_up, layer)
                )
            else:
                after = stash[layer + 1][s][0]
                got = mlp_back(None, after, d_mid[s], sent[s], vec, slope, w_down, w_up, layer)
            grad.append(got[0])
            d_mlp.append(got[1])
            d_pre.append(got[2])
            ups.append(got[5])
            mlp.append(got[6])
            sent[s] = send_part(got[3], got[4])
        g_down = both_t_mm([k[7] for k in kept], d_mlp)
        g_up = both_t_mm([k[5] for k in kept], d_pre)
        for s in streams:
            _, _, qkv, _, mid, _, _, _, stat = kept[s]
            got = attend_back(
                grad[s], mid, sent[s], vec, qkv, stat, w_proj, w_qkv, layer, heads, size
            )
            d_mid[s] = got[0]
            d_branch.append(got[1])
            d_joined.append(got[2])
            att.append(got[5])
            joined.append(got[6])
            sent[s] = send_part(got[3], got[4])
        g_proj = both_t_mm([k[3] for k in kept], d_branch)
        g_qkv = both_t_mm([k[1] for k in kept], d_joined)
        grads[layer] = (g_qkv, g_proj, g_up, g_down)
        tallies[layer] = [*ups, *mlp, *att, *joined]
    ends = [(stash[0][s][0], d_mid[s], *sent[s]) for s in streams]
    input_grad, first = last_back(where, ends, vec)
    input_grad = input_grad[None]

    if fast:
        tiny = call(
            functools.partial(pack_body, n, heads, size),
            [((n, 24, 2 * rows), f32)],
            [where, first, *tallies[1], *tallies[0]],
            0,
            smem=1,
        )[0]
        tiny = scatter(tiny.reshape(n * 24, 2 * rows), where, f, n)
        tiny = (tiny[0] + tiny[1]) + (tiny[2] + tiny[3])
        tiny = tiny + core_swap(tiny)
        tiny = tiny + y_swap(tiny)
        vecs = pick(tiny[:16].reshape(8, LAYERS, 2, rows), 2, c)
        ups = pick(tiny[16:].reshape(LAYERS, 2, 2 * 2 * rows), 1, c)
        outs = None
        for layer in reversed(range(LAYERS)):
            g_qkv, g_proj, g_up, g_down = grads[layer]
            d = both_types(scatter(g_down, where, f, n))
            d = (d[0], y_swap(d[1]))
            u = scatter(g_up, where, f, n)
            u = to_rows(u, where)
            q = to_rows(scatter(g_qkv, where, f, n), where)
            p = both_types(scatter(g_proj, where, f, n, True))
            side = x_swap(p[1], n)
            p = both_types([p[0], side])
            p = (p[0], y_swap(p[1]))
            outs = finish(where, q, u, d, p, outs, layer, n, heads, size)
        qkv_out, proj_out, up_out, down_out = outs
    else:
        here = (jnp.arange(4) == quarter).reshape(1, 1, 4, 1)
        at_c = (jnp.arange(2) == c).reshape(1, 2, 1, 1)
        at_y = (jnp.arange(2) == y).reshape(1, 1, 2, 1)

        def rows_of(pair, i):
            return jnp.sum(pair[0][8 * i : 8 * i + 8] + pair[1][8 * i : 8 * i + 8], axis=0)

        by_owner = []
        for layer in range(LAYERS):
            tally = tallies[layer]
            ups, mlp, att, joined = [tally[2 * i : 2 * i + 2] for i in range(4)]
            if layer == 0:
                one_sums = [jnp.sum(first[8 * i : 8 * i + 8], axis=0) for i in range(2)]
            else:
                one_sums = [rows_of(tallies[layer - 1][2:4], i) for i in range(2)]
            joined = rows_of(joined, 0).reshape(3, heads, 1, size)[0::2]
            joined = jnp.where(here, joined, 0.0).reshape(2, width)
            alike = [rows_of(mlp, 2), *one_sums, rows_of(att, 2), rows_of(att, 0), rows_of(att, 1)]
            alike = [0.25 * v for v in alike]
            vecs = [alike[1], alike[2], joined[0], joined[1], alike[3], alike[4], alike[5], alike[0]]
            vecs = jnp.stack(vecs).reshape(8, 2 * n, rows).transpose(1, 0, 2)
            up = rows_of(ups, 0).reshape(n, 1, 1, hid_rows // 2)
            up = jnp.where(at_c & at_y, up, 0.0).reshape(2 * n, hid_rows)
            by_owner.append(jnp.concatenate([vecs.reshape(2 * n, 8 * rows), up], axis=1))
        total = lax.psum(jnp.stack(by_owner, axis=1), ("fsdp", "seq", "replica"))
        tiny = pick(total, 0, 2 * f + c)
        vecs = tiny[:, : 8 * rows].reshape(LAYERS, 8, rows).transpose(1, 0, 2)
        ups = tiny[:, 8 * rows :]
        axes = ("replica", "seq")

        def owned(full):
            block = lax.psum_scatter(full, "fsdp", scatter_dimension=0, tiled=True)
            half = block.shape[0] // 2
            return widen(lax.dynamic_slice_in_dim(block, c * half, half, axis=0))

        outs = []
        for layer in range(LAYERS):
            g_qkv, g_proj, g_up, g_down = grads[layer]
            g = lax.all_gather(g_qkv, axes, axis=0).reshape(4, width, 3, heads, size)
            qkv_out = owned(g.transpose(1, 2, 3, 0, 4).reshape(width, 3 * width))
            g = lax.all_gather(g_proj, axes, axis=0).reshape(4, heads, size, width)
            proj_out = owned(g.transpose(1, 0, 2, 3).reshape(width, width))
            g = lax.all_gather(g_up, axes, axis=0)
            g = g.reshape(2, 2, width, n, hid_rows // 2)
            up_out = owned(g.transpose(2, 3, 1, 0, 4).reshape(width, hidden))
            g = lax.all_gather(g_down, axes, axis=0)
            g = g.reshape(2, 2, n, hid_rows // 2, width)
            down_out = owned(g.transpose(2, 1, 0, 3, 4).reshape(hidden, width))
            outs.append((qkv_out, proj_out, up_out, down_out))
        qkv_out, proj_out, up_out, down_out = [
            jnp.stack([outs[layer][i] for layer in range(LAYERS)]) for i in range(4)
        ]
    return (
        clips_out,
        input_grad,
        vecs[GAIN_ONE],
        vecs[SHIFT_ONE],
        qkv_out,
        vecs[QUERY_B],
        vecs[VALUE_B],
        proj_out,
        vecs[PROJ_B],
        vecs[GAIN_TWO],
        vecs[SHIFT_TWO],
        up_out,
        ups,
        down_out,
        vecs[DOWN_B],
    )


def solution(mesh):
    tokens = P(("fsdp", "replica"), "seq", None)
    vector = P(None, ("fsdp", "seq"))
    matrix = P(None, ("fsdp", "seq"), None)
    kinds = [
        vector,
        vector,
        matrix,
        vector,
        vector,
        matrix,
        vector,
        vector,
        vector,
        matrix,
        vector,
        matrix,
        vector,
    ]
    return jax.shard_map(
        functools.partial(on_device, n=mesh.shape["fsdp"]),
        mesh=mesh,
        in_specs=(tokens, tokens, P(("fsdp", "replica")), *kinds),
        out_specs=(tokens, tokens, *kinds),
        check_vma=False,
    )
```
